768 devices in a mesh: lat: 48 (over z, y_hi), lon: 16 (over y_lo, x, core).
Axes of the slice: x: 4, y: 8 (y_hi: 4, y_lo: 2; y = y_hi * 2 + y_lo), z: 12, core: 2. Of those that a mesh axis runs over, the one named last changes fastest.
Arguments:
- initial_state: float32 [6, 2304, 2048], P(None, 'lat', 'lon'), may hold values from -6 to 6
- source: float32 [6, 2304, 2048], P(None, 'lat', 'lon'), may hold values from -3 to 3
- cotangent: float32 [6, 2304, 2048], P(None, 'lat', 'lon'), may hold values from -6 to 6
- face_coefs: float32 [2, 2304, 2048], P(None, 'lat', 'lon'), may hold values from 0.03 to 0.1
- land_mask: int32 [6, 2304, 2048], P(None, 'lat', 'lon'), may hold values 0 or 1
- bottom: int32 [2304, 2048], P('lat', 'lon'), may hold values from 1 to 6
Outputs:
- final_state: float32 [6, 2304, 2048], P(None, 'lat', 'lon')
- grad_initial: float32 [6, 2304, 2048], P(None, 'lat', 'lon')
- grad_source: float32 [6, 2304, 2048], P(None, 'lat', 'lon')
The draws below stay inside these ranges and needn't reach their ends.
All inputs are finite; a program needn't handle non-finite values. No bound on the sum of `land_mask` on one device may be relied on, other than what follows from the above.
Results may differ from the reference program's by a relative error of at most 0.00002.
Values sent between devices are 32-bit elements; how exact they have to be, the bound alone decides.
A program may use at most 32 MiB of HBM per device.

```python
import math
import jax
import jax.numpy as jnp
from jax import lax

K = 6
STEPS = 4
NLAT = 2304
NLON = 2048


def touch_ends(entries, stream_key, least, top_value):
    index_at = [jax.random.randint(jax.random.fold_in(stream_key, axis), (), 0, length) for axis, length in enumerate(entries.shape)]
    widest = entries.shape.index(max(entries.shape))
    neighbour = index_at[:widest] + [(index_at[widest] + 1) % entries.shape[widest]] + index_at[widest + 1:]
    return entries.at[tuple(index_at)].set(least).at[tuple(neighbour)].set(top_value)


def shard_levels(own_key, dims, split, least, top_value):
    def one(dim, shards_of):
        draws = jax.random.uniform(jax.random.fold_in(jax.random.fold_in(own_key, 6), dim), (shards_of,), jnp.float32, least / len(split), top_value / len(split))
        return jnp.repeat(jnp.exp(draws), dims[dim] // shards_of).reshape((-1,) + (1,) * (len(dims) - dim - 1))

    loudness = one(*split[0])
    for cut in split[1:]:
        loudness = loudness * one(*cut)
    return loudness


def noise(rng, extent, width, bound, pieces=(), held_as=jnp.bfloat16):
    drawn = width * jax.random.normal(rng, extent, jnp.float32)
    if pieces:
        drawn = drawn * shard_levels(rng, extent, pieces, -0.22, 0.18)
    return jnp.clip(drawn, -bound, bound).astype(held_as)


def setup_inputs(seed: int = 0) -> dict:
    key_of = jax.random.split(jax.random.key(seed), 7)
    initial_state = noise(key_of[0], (K, NLAT, NLON), 1.0, 6.0, ((1, 48), (2, 16)), jnp.float32)
    source = noise(key_of[1], (K, NLAT, NLON), 0.5, 3.0, ((1, 48), (2, 16)), jnp.float32)
    cotangent = noise(key_of[2], (K, NLAT, NLON), 1.0, 6.0, ((1, 48), (2, 16)), jnp.float32)
    face_coefs = jnp.clip(jnp.exp(math.log(0.1) - 1.2039728 * jax.random.uniform(key_of[3], (2, NLAT, NLON), jnp.float32) ** shard_levels(key_of[3], (2, NLAT, NLON), ((1, 48), (2, 16)), -0.2, 0.2)), 0.03, 0.1)
    land_mask = touch_ends((jax.random.randint(key_of[4], (K, NLAT, NLON), 0, 5) < 4).astype(jnp.int32), jax.random.fold_in(key_of[4], 1), 0, 1)
    bottom = touch_ends(jax.random.randint(key_of[5], (NLAT, NLON), 1, K + 1), jax.random.fold_in(key_of[5], 1), 1, K).astype(jnp.int32)
    return dict(initial_state=initial_state, source=source, cotangent=cotangent, face_coefs=face_coefs, land_mask=land_mask, bottom=bottom)


vertical_coef = 0.04

def wet_cells(land_mask, bottom):
    levels = lax.broadcasted_iota(jnp.int32, land_mask.shape, 0)
    return jnp.where(levels < bottom[None, :, :], land_mask, 0).astype(jnp.float32)

def operate(values, wet_mask, coef_lon, coef_lat):
    east_values = jnp.roll(values, -1, axis=2)
    wet_east = jnp.roll(wet_mask, -1, axis=2)
    flux_east = coef_lon[None] * (wet_mask * wet_east) * (east_values - values)
    north_values = jnp.roll(values, -1, axis=1)
    wet_north = jnp.roll(wet_mask, -1, axis=1)
    flux_north = coef_lat[None] * (wet_mask * wet_north) * (north_values - values)
    flux_up = vertical_coef * (wet_mask[:-1] * wet_mask[1:]) * (values[1:] - values[:-1])
    zero_level = jnp.zeros_like(values[:1])
    vertical = jnp.concatenate([flux_up, zero_level], 0) - jnp.concatenate([zero_level, flux_up], 0)
    east_part = flux_east - jnp.roll(flux_east, 1, axis=2)
    north_part = flux_north - jnp.roll(flux_north, 1, axis=1)
    return values + east_part + north_part + vertical

def reference(initial_state, source, cotangent, face_coefs, land_mask, bottom):
    wet_mask = wet_cells(land_mask, bottom)
    row_index = lax.broadcasted_iota(jnp.int32, face_coefs.shape[1:], 0)
    coef_lat = jnp.where(row_index < NLAT - 1, face_coefs[1], jnp.float32(0.0))
    coef_lon = face_coefs[0]

    def forward(initial, forcing):
        tracer = initial
        for step_index in range(STEPS):
            tracer = wet_mask * (jnp.tanh(operate(tracer, wet_mask, coef_lon, coef_lat)) + forcing)
        return tracer
    final_state, pullback = jax.vjp(forward, initial_state, source)
    grad_initial, grad_source = pullback(cotangent)
    return (final_state, grad_initial, grad_source)
```

```python
import jax
import jax.numpy as jnp
from jax import lax
from jax.experimental import pallas as pl
from jax.experimental.pallas import tpu as pltpu
from jax.sharding import PartitionSpec as P

MESH = pl.DeviceIdType.MESH
STEPS = 4
K = 6
ROWS = 48
LANES = 128
TILES = 8
PAD = 80
VERTICAL = 0.04
F32 = jnp.float32

STATE, WET, SOURCE, COEF, COT = 0, 6, 12, 18, 20
PLANES = 26
PAIRS = PLANES // 2


def lane_roll(x, shift):
    return pltpu.roll(x, shift % LANES, x.ndim - 1)


def kernel(
    state_hbm, source_hbm, cot_hbm, coef_hbm, mask_hbm, bottom_hbm,
    final_ref, gini_ref, gsrc_ref,
    u_a, u_b, wet, src, cot, coef, mask, bottom,
    c_e, c_w, c_n, c_z, diag, gain,
    packed, pack_e, pack_w, corner_out, got_w, got_e, corner_in,
    s_a, s_b, s_c, s_src, s_cot, s_gain,
    load_sem, send_sem, recv_sem,
):
    lat, lon = lax.axis_index("lat"), lax.axis_index("lon")
    n_lat, n_lon = lax.axis_size("lat"), lax.axis_size("lon")
    up, down = lax.rem(lat + 1, n_lat), lax.rem(lat + n_lat - 1, n_lat)
    east, west = lax.rem(lon + 1, n_lon), lax.rem(lon + n_lon - 1, n_lon)
    neighbours = [
        (up, lon), (down, lon), (lat, east), (lat, west),
        (up, east), (up, west), (down, east), (down, west),
    ]

    lane = lax.broadcasted_iota(jnp.int32, (1, 8, LANES), 2)
    sub = lax.broadcasted_iota(jnp.int32, (1, 8, LANES), 1)
    block = lane // 16
    left = lane % 16 < 8
    own = pl.ds(16, ROWS)

    loads = [
        pltpu.make_async_copy(src_ref, dst_ref, load_sem.at[i])
        for i, (src_ref, dst_ref) in enumerate(
            [
                (bottom_hbm, bottom),
                (mask_hbm, mask),
                (coef_hbm, coef.at[:, own]),
                (state_hbm, u_a.at[:, own]),
                (source_hbm, src.at[:, own]),
                (cot_hbm, cot.at[:, own]),
            ]
        )
    ]
    for load in loads:
        load.start()

    zero_tile = jnp.zeros((K, 8, LANES), F32)
    for ref in (u_a, u_b, wet):
        ref[:, 0:8] = zero_tile
        ref[:, 72:80] = zero_tile
    coef[:, 0:8] = zero_tile[:2]
    coef[:, 72:80] = zero_tile[:2]
    c_n[:, 0:8] = zero_tile
    packed[:, :, :] = jnp.zeros((PLANES, 8, LANES), F32)

    barrier = pltpu.get_barrier_semaphore()
    for device in neighbours:
        pl.semaphore_signal(barrier, inc=1, device_id=device, device_id_type=MESH)

    def pack_own(values, plane, count):
        for k in range(count):
            total = packed[plane + k : plane + k + 1]
            for j in range(6):
                moved = lane_roll(values(k, j), 16 * (j + 1) + 8)
                total = jnp.where(block == j + 1, moved, total)
            packed[plane + k : plane + k + 1] = total

    loads[0].wait()
    loads[1].wait()
    for k in range(K):
        wet[k, 16 : 16 + ROWS] = jnp.where(k < bottom[...], mask[k], 0).astype(F32)
    loads[2].wait()
    closed = jnp.logical_and(sub == 7, lat == n_lat - 1)
    coef[1:2, 56:64] = jnp.where(closed, 0.0, coef[1:2, 56:64])

    def tile_of(ref):
        return lambda k, j: ref[k : k + 1, 16 + 8 * j : 24 + 8 * j]

    pack_own(tile_of(wet), WET, K)
    pack_own(tile_of(coef), COEF, 2)
    loads[3].wait()
    pack_own(tile_of(u_a), STATE, K)
    loads[4].wait()
    pack_own(tile_of(src), SOURCE, K)
    loads[5].wait()
    pack_own(tile_of(cot), COT, K)

    for i in range(PAIRS):
        first, second = packed[2 * i : 2 * i + 1], packed[2 * i + 1 : 2 * i + 2]
        pack_e[i : i + 1] = jnp.where(left, first, lane_roll(second, 8))
        pack_w[i : i + 1] = jnp.where(left, lane_roll(first, -8), second)
    for c, (ref, source_block) in enumerate(((pack_e, 6), (pack_w, 6), (pack_e, 1), (pack_w, 1))):
        for v in range(2):
            total = jnp.zeros((1, 8, LANES), F32)
            for j in range(min(8, PAIRS - 8 * v)):
                i = 8 * v + j
                moved = lane_roll(ref[i : i + 1], 16 * (j - source_block))
                total = jnp.where(block == j, moved, total)
            corner_out[c, v : v + 1] = total

    pl.semaphore_wait(barrier, len(neighbours))

    copies = []

    def send(src_ref, dst_ref, device):
        i = len(copies)
        copy = pltpu.make_async_remote_copy(
            src_ref=src_ref, dst_ref=dst_ref, send_sem=send_sem.at[i], recv_sem=recv_sem.at[i],
            device_id=device, device_id_type=MESH,
        )
        copy.start()
        copies.append(copy)
        return copy

    top, bot = pl.ds(56, 8), pl.ds(16, 8)
    low, high = pl.ds(8, 8), pl.ds(64, 8)
    corners = [
        send(corner_out.at[c], corner_in.at[c], device)
        for c, device in enumerate(((up, east), (up, west), (down, east), (down, west)))
    ]
    strips = [send(pack_e, got_w, (lat, east)), send(pack_w, got_e, (lat, west))]
    rows = {}
    for name, ref in (("wet", wet), ("coef", coef), ("state", u_a), ("src", src), ("cot", cot)):
        rows[name] = [
            send(ref.at[:, top], ref.at[:, low], (up, lon)),
            send(ref.at[:, bot], ref.at[:, high], (down, lon)),
        ]

    for copy in corners + strips:
        copy.wait_recv()
    for ref, low_corner, high_corner in ((got_w, 0, 2), (got_e, 1, 3)):
        for i in range(PAIRS):
            v, j = i // 8, i % 8
            total = ref[i : i + 1]
            total = jnp.where(block == 0, lane_roll(corner_in[low_corner, v : v + 1], -16 * j), total)
            total = jnp.where(block == 7, lane_roll(corner_in[high_corner, v : v + 1], 16 * (7 - j)), total)
            ref[i : i + 1] = total

    for name in rows:
        for copy in rows[name]:
            copy.wait_recv()
    for copy in copies:
        copy.wait_send()

    for plane, ref, count in ((STATE, u_a, K), (WET, wet, K), (SOURCE, src, K), (COEF, coef, 2), (COT, cot, K)):
        for k in range(count):
            total = packed[plane + k : plane + k + 1]
            total = jnp.where(block == 0, lane_roll(ref[k : k + 1, 8:16], 8), total)
            total = jnp.where(block == 7, lane_roll(ref[k : k + 1, 64:72], 120), total)
            packed[plane + k : plane + k + 1] = total

    def strip(plane):
        i = plane // 2
        mine, from_west, from_east = packed[plane : plane + 1], got_w[i : i + 1], got_e[i : i + 1]
        if plane % 2 == 0:
            return jnp.where(left, from_west, mine), jnp.where(left, mine, lane_roll(from_east, 8))
        return jnp.where(left, lane_roll(from_west, -8), mine), jnp.where(left, mine, from_east)

    def strips_of(plane, count):
        return jnp.concatenate([part for k in range(count) for part in strip(plane + k)], 0)

    def s_north(x):
        rolled = pltpu.roll(x, 7, 1)
        return jnp.where(sub == 7, lane_roll(rolled, -16), rolled)

    def s_south(x):
        rolled = pltpu.roll(x, 1, 1)
        return jnp.where(sub == 0, lane_roll(rolled, 16), rolled)

    def joined(x):
        return [jnp.where(left, x[2 * k : 2 * k + 1], x[2 * k + 1 : 2 * k + 2]) for k in range(x.shape[0] // 2)]

    def beside(x, outer, r):
        turned = lane_roll(outer, 120 - 16 * r)
        return (
            lane_roll(jnp.where(lane == 0, turned, x), -1),
            lane_roll(jnp.where(lane == LANES - 1, turned, x), 1),
        )

    def six(x, y):
        return jnp.concatenate([x, y] * K, 0)

    w = strips_of(WET, K)
    coef_e, coef_n = strips_of(COEF, 2)[0:2], strips_of(COEF, 2)[2:4]
    all_e, all_n = six(coef_e[0:1], coef_e[1:2]), six(coef_n[0:1], coef_n[1:2])
    s_ce = all_e * w * lane_roll(w, -1)
    s_cw = lane_roll(all_e, 1) * lane_roll(w, 1) * w
    s_cn = all_n * w * s_north(w)
    s_cs = s_south(all_n) * s_south(w) * w
    s_cz = VERTICAL * (w[:-2] * w[2:])
    nothing = jnp.zeros((2, 8, LANES), F32)
    s_d = 1.0 - (s_ce + s_cw) - (s_cn + s_cs)
    s_d = s_d - jnp.concatenate([s_cz, nothing], 0) - jnp.concatenate([nothing, s_cz], 0)
    for i, part in enumerate((s_d, s_ce, s_cw, s_cn, s_cs)):
        s_c[i] = part
    s_c[5, 0:10] = s_cz
    s_src[...] = strips_of(SOURCE, K)
    s_cot[...] = strips_of(COT, K)
    s_a[...] = strips_of(STATE, K)
    wet_outer = joined(w)
    coef_outer = joined(coef_e)[0]

    for r in range(TILES):
        at = 8 + 8 * r
        ce, cn, cs = coef[0:1, at : at + 8], coef[1:2, at : at + 8], coef[1:2, at - 1 : at + 7]
        _, ce_west = beside(ce, coef_outer, r)
        tiles = [wet[k : k + 1, at : at + 8] for k in range(K)]
        below = None
        for k in range(K):
            wk = tiles[k]
            w_east, w_west = beside(wk, wet_outer[k], r)
            e, wst = ce * wk * w_east, ce_west * w_west * wk
            n = cn * wk * wet[k : k + 1, at + 1 : at + 9]
            s = cs * wet[k : k + 1, at - 1 : at + 7] * wk
            d = 1.0 - (e + wst) - (n + s)
            if k < K - 1:
                z = VERTICAL * (wk * tiles[k + 1])
                c_z[k : k + 1, 8 * r : 8 * r + 8] = z
                d = d - z
            if below is not None:
                d = d - below
            below = z
            c_e[k : k + 1, 8 * r : 8 * r + 8] = e
            c_w[k : k + 1, 8 * r : 8 * r + 8] = wst
            c_n[k : k + 1, at : at + 8] = n
            diag[k : k + 1, 8 * r : 8 * r + 8] = d

    def strip_product(ref):
        x = ref[...]
        out = s_c[0] * x + (s_c[1] * lane_roll(x, -1) + s_c[2] * lane_roll(x, 1))
        out = out + (s_c[3] * s_north(x) + s_c[4] * s_south(x))
        cz = s_c[5, 0:10]
        out = out + jnp.concatenate([cz * x[2:], nothing], 0) + jnp.concatenate([nothing, cz * x[:-2]], 0)
        return out, joined(x)

    def product(ref, outer, r):
        at, t = 8 + 8 * r, 8 * r
        x = [ref[k : k + 1, at : at + 8] for k in range(K)]
        out = []
        for k in range(K):
            x_east, x_west = beside(x[k], outer[k], r)
            p = diag[k : k + 1, t : t + 8] * x[k]
            p = p + (c_e[k : k + 1, t : t + 8] * x_east + c_w[k : k + 1, t : t + 8] * x_west)
            p = p + (
                c_n[k : k + 1, at : at + 8] * ref[k : k + 1, at + 1 : at + 9]
                + c_n[k : k + 1, at - 1 : at + 7] * ref[k : k + 1, at - 1 : at + 7]
            )
            if k < K - 1:
                p = p + c_z[k : k + 1, t : t + 8] * x[k + 1]
            if k > 0:
                p = p + c_z[k - 1 : k, t : t + 8] * x[k - 1]
            out.append(p)
        return out

    def forward(n, now, later, s_now, s_later):
        p, outer = strip_product(s_now)
        bounded = jnp.tanh(p)
        s_gain[n] = 1.0 - bounded * bounded
        s_later[...] = bounded + s_src[...]
        for r in range(TILES):
            at = 8 + 8 * r
            for k, p in enumerate(product(now, outer, r)):
                bounded = jnp.tanh(p)
                gain[n, k : k + 1, 8 * r : 8 * r + 8] = 1.0 - bounded * bounded
                later[k : k + 1, at : at + 8] = bounded + src[k : k + 1, at : at + 8]

    def forward_two(i, carry):
        forward(2 * i, u_a, u_b, s_a, s_b)
        forward(2 * i + 1, u_b, u_a, s_b, s_a)
        return carry

    lax.fori_loop(0, STEPS // 2, forward_two, 0)

    for r in range(TILES):
        at = 8 + 8 * r
        for k in range(K):
            if 1 <= r <= 6:
                o = 8 * r - 8
                final_ref[k : k + 1, o : o + 8] = wet[k : k + 1, at : at + 8] * u_a[k : k + 1, at : at + 8]
                gsrc_ref[k : k + 1, o : o + 8] = cot[k : k + 1, at : at + 8]
            u_a[k : k + 1, at : at + 8] = gain[STEPS - 1, k : k + 1, 8 * r : 8 * r + 8] * cot[k : k + 1, at : at + 8]
    s_a[...] = s_gain[STEPS - 1] * s_cot[...]

    def backward(n, now, later, s_now, s_later):
        p, outer = strip_product(s_now)
        s_later[...] = s_gain[n - 1] * p
        for r in range(TILES):
            at = 8 + 8 * r
            for k, p in enumerate(product(now, outer, r)):
                later[k : k + 1, at : at + 8] = gain[n - 1, k : k + 1, 8 * r : 8 * r + 8] * p
                if 1 <= r <= 6:
                    o = 8 * r - 8
                    gsrc_ref[k : k + 1, o : o + 8] += p

    backward(3, u_a, u_b, s_a, s_b)
    backward(2, u_b, u_a, s_b, s_a)
    backward(1, u_a, u_b, s_a, s_b)
    outer = joined(s_b[...])
    for r in range(1, 7):
        at, o = 8 + 8 * r, 8 * r - 8
        for k, p in enumerate(product(u_b, outer, r)):
            w = wet[k : k + 1, at : at + 8]
            gini_ref[k : k + 1, o : o + 8] = w * p
            gsrc_ref[k : k + 1, o : o + 8] = w * gsrc_ref[k : k + 1, o : o + 8]


def body(initial_state, source, cotangent, face_coefs, land_mask, bottom):
    out = jax.ShapeDtypeStruct((K, ROWS, LANES), F32)
    rows = pltpu.VMEM((K, PAD, LANES), F32)
    tiles = pltpu.VMEM((K, 8 * TILES, LANES), F32)
    strips = pltpu.VMEM((2 * K, 8, LANES), F32)
    pairs = pltpu.VMEM((PAIRS, 8, LANES), F32)
    return pl.pallas_call(
        kernel,
        name="window",
        out_shape=(out, out, out),
        in_specs=[pl.BlockSpec(memory_space=pl.ANY)] * 6,
        out_specs=(pl.BlockSpec(memory_space=pltpu.VMEM),) * 3,
        scratch_shapes=[
            rows, rows, rows, rows, rows,
            pltpu.VMEM((2, PAD, LANES), F32),
            pltpu.VMEM((K, ROWS, LANES), jnp.int32),
            pltpu.VMEM((ROWS, LANES), jnp.int32),
            tiles, tiles, rows, tiles, tiles,
            pltpu.VMEM((STEPS, K, 8 * TILES, LANES), F32),
            pltpu.VMEM((PLANES, 8, LANES), F32),
            pairs, pairs,
            pltpu.VMEM((4, 2, 8, LANES), F32),
            pairs, pairs,
            pltpu.VMEM((4, 2, 8, LANES), F32),
            strips, strips,
            pltpu.VMEM((6, 2 * K, 8, LANES), F32),
            strips, strips,
            pltpu.VMEM((STEPS, 2 * K, 8, LANES), F32),
            pltpu.SemaphoreType.DMA((6,)),
            pltpu.SemaphoreType.DMA((16,)),
            pltpu.SemaphoreType.DMA((16,)),
        ],
        compiler_params=pltpu.CompilerParams(collective_id=0, has_side_effects=True),
    )(initial_state, source, cotangent, face_coefs, land_mask, bottom)


def solution(mesh):
    spec = P(None, "lat", "lon")
    return jax.shard_map(
        body,
        mesh=mesh,
        in_specs=(spec,) * 5 + (P("lat", "lon"),),
        out_specs=(spec,) * 3,
        check_vma=False,
    )
```

```python
import jax
import jax.numpy as jnp
from jax import lax
from jax.experimental import pallas as pl
from jax.experimental.pallas import tpu as pltpu
from jax.sharding import PartitionSpec as P

MESH = pl.DeviceIdType.MESH
STEPS = 4
K = 6
ROWS = 48
LANES = 128
TILES = 8
PAD = 80
UNROLL = 8
PAIR_UNROLL = 7
COEF_UNROLL = 2
VERTICAL = 0.04
F32 = jnp.float32

STATE, WET, SOURCE, COEF, COT, OTHER = 0, 6, 12, 18, 20, 26
PLANES = 26
PAIRS = PLANES // 2 + 1


def lane_roll(x, shift):
    if isinstance(shift, int):
        shift %= LANES
    return pltpu.roll(x, shift, x.ndim - 1)


def kernel(
    state_hbm, source_hbm, cot_hbm, coef_hbm, mask_hbm, bottom_hbm,
    final_ref, gini_ref, gsrc_ref,
    x_ref, mask, bottom,
    c_e, c_w, c_n, c_z, diag, gain, adj,
    packed, pack_e, pack_w, corner_out, got_w, got_e, corner_in,
    s_ref, s_c, s_gain,
    load_sem, send_sem, recv_sem,
):
    lat, lon = lax.axis_index("lat"), lax.axis_index("lon")
    n_lat, n_lon = lax.axis_size("lat"), lax.axis_size("lon")
    up, down = lax.rem(lat + 1, n_lat), lax.rem(lat + n_lat - 1, n_lat)
    east, west = lax.rem(lon + 1, n_lon), lax.rem(lon + n_lon - 1, n_lon)
    neighbours = [
        (up, lon), (down, lon), (lat, east), (lat, west),
        (up, east), (up, west), (down, east), (down, west),
    ]

    barrier = pltpu.get_barrier_semaphore()
    for device in neighbours:
        pl.semaphore_signal(barrier, inc=1, device_id=device, device_id_type=MESH)

    lane = lax.broadcasted_iota(jnp.int32, (1, 8, LANES), 2)
    sub = lax.broadcasted_iota(jnp.int32, (1, 8, LANES), 1)
    block = lane // 16
    left = lane % 16 < 8
    own = pl.ds(16, ROWS)

    def planes(start, count):
        return x_ref.at[pl.ds(start, count)]

    fields = [
        (mask_hbm, mask, 8),
        (bottom_hbm, bottom, 8),
        (coef_hbm, planes(COEF, 2), 16),
        (state_hbm, planes(STATE, K), 16),
        (source_hbm, planes(SOURCE, K), 16),
        (cot_hbm, planes(COT, K), 16),
    ]

    def rows_of(ref, start, size):
        if len(ref.shape) == 2:
            return ref.at[pl.ds(start, size)]
        return ref.at[:, pl.ds(start, size)]

    loads = [
        pltpu.make_async_copy(hbm, rows_of(ref, first, ROWS), load_sem.at[i])
        for i, (hbm, ref, first) in enumerate(fields)
    ]
    for load in loads:
        load.start()

    zero_tile = jnp.zeros((1, 8, LANES), F32)

    def clear(p, carry):
        x_ref[pl.ds(p, 1), 0:8] = zero_tile
        x_ref[pl.ds(p, 1), 72:80] = zero_tile
        return carry

    lax.fori_loop(0, PLANES + K, clear, 0)
    c_n[:, 0:8] = jnp.zeros((K, 8, LANES), F32)

    pl.semaphore_wait(barrier, len(neighbours))

    copies = []

    def send(src_ref, dst_ref, device):
        i = len(copies)
        copy = pltpu.make_async_remote_copy(
            src_ref=src_ref, dst_ref=dst_ref, send_sem=send_sem.at[i], recv_sem=recv_sem.at[i],
            device_id=device, device_id_type=MESH,
        )
        copy.start()
        copies.append(copy)
        return copy

    rows = []
    for hbm, ref, first in fields:
        rows.append(send(rows_of(hbm, ROWS - 8, 8), rows_of(ref, first - 8, 8), (up, lon)))
        rows.append(send(rows_of(hbm, 0, 8), rows_of(ref, first + ROWS, 8), (down, lon)))

    def wet_rows(start, size):
        for k in range(K):
            here = pl.ds(start, size)
            x_ref[WET + k, pl.ds(start + 8, size)] = jnp.where(k < bottom[here], mask[k, here], 0).astype(F32)

    def close(at, condition):
        tile = x_ref[COEF + 1 : COEF + 2, at : at + 8]
        x_ref[COEF + 1 : COEF + 2, at : at + 8] = jnp.where(jnp.logical_and(sub == 7, condition), 0.0, tile)

    for load in loads:
        load.wait()
    wet_rows(8, ROWS)
    close(56, lat == n_lat - 1)

    def by_pair(one):
        def several(i, carry):
            for q in range(PAIR_UNROLL):
                one(i * PAIR_UNROLL + q)
            return carry

        lax.fori_loop(0, PAIRS // PAIR_UNROLL, several, 0)

    def pack(i):
        both = []
        for q in range(2):
            total = zero_tile
            for j in range(6):
                moved = lane_roll(x_ref[pl.ds(2 * i + q, 1), 16 + 8 * j : 24 + 8 * j], 16 * (j + 1) + 8)
                total = moved if j == 0 else jnp.where(block == j + 1, moved, total)
            packed[pl.ds(2 * i + q, 1)] = total
            both.append(total)
        to_east = jnp.where(left, both[0], lane_roll(both[1], 8))
        to_west = jnp.where(left, lane_roll(both[0], -8), both[1])
        pack_e[pl.ds(i, 1)] = to_east
        pack_w[pl.ds(i, 1)] = to_west
        v, j = i // 8, i % 8
        for c, (value, source_block) in enumerate(((to_east, 6), (to_west, 6), (to_east, 1), (to_west, 1))):
            moved = lane_roll(value, lax.rem(16 * (j + 8 - source_block), LANES))
            corner_out[c, pl.ds(v, 1)] = jnp.where(block == j, moved, corner_out[c, pl.ds(v, 1)])

    by_pair(pack)

    corners = [
        send(corner_out.at[c], corner_in.at[c], device)
        for c, device in enumerate(((up, east), (up, west), (down, east), (down, west)))
    ]
    strips = [send(pack_e, got_w, (lat, east)), send(pack_w, got_e, (lat, west))]

    for copy in rows:
        copy.wait_recv()
    wet_rows(0, 8)
    wet_rows(ROWS + 8, 8)
    close(8, lat == 0)
    for copy in corners + strips:
        copy.wait_recv()

    def unpack(i):
        v, j = i // 8, i % 8
        sides = []
        for ref, low, high in ((got_w, 0, 2), (got_e, 1, 3)):
            total = ref[pl.ds(i, 1)]
            total = jnp.where(block == 0, lane_roll(corner_in[low, pl.ds(v, 1)], lax.rem(LANES - 16 * j, LANES)), total)
            total = jnp.where(block == 7, lane_roll(corner_in[high, pl.ds(v, 1)], 16 * (7 - j)), total)
            sides.append(total)
        from_west, from_east = sides
        for q in range(2):
            p = 2 * i + q
            mine = packed[pl.ds(p, 1)]
            mine = jnp.where(block == 0, lane_roll(x_ref[pl.ds(p, 1), 8:16], 8), mine)
            mine = jnp.where(block == 7, lane_roll(x_ref[pl.ds(p, 1), 64:72], 120), mine)
            a = from_west if q == 0 else lane_roll(from_west, -8)
            b = lane_roll(from_east, 8) if q == 0 else from_east
            s_ref[pl.ds(2 * p, 1)] = jnp.where(left, a, mine)
            s_ref[pl.ds(2 * p + 1, 1)] = jnp.where(left, mine, b)

    by_pair(unpack)

    def s_north(x):
        rolled = pltpu.roll(x, 7, 1)
        return jnp.where(sub == 7, lane_roll(rolled, -16), rolled)

    def s_south(x):
        rolled = pltpu.roll(x, 1, 1)
        return jnp.where(sub == 0, lane_roll(rolled, 16), rolled)

    def beside(x, a, b, r):
        turned = lane_roll(jnp.where(left, a, b), lax.rem(120 + LANES - 16 * r, LANES))
        return (
            lane_roll(jnp.where(lane == 0, turned, x), -1),
            lane_roll(jnp.where(lane == LANES - 1, turned, x), 1),
        )

    def level(p):
        return s_ref[2 * p : 2 * p + 1], s_ref[2 * p + 1 : 2 * p + 2]

    def six(pair):
        return jnp.concatenate([pair] * K, 0)

    w = s_ref[2 * WET : 2 * WET + 2 * K]
    all_e = six(s_ref[2 * COEF : 2 * COEF + 2])
    all_n = six(s_ref[2 * COEF + 2 : 2 * COEF + 4])
    s_ce = all_e * w * lane_roll(w, -1)
    s_cw = lane_roll(all_e, 1) * lane_roll(w, 1) * w
    s_cn = all_n * w * s_north(w)
    s_cs = s_south(all_n) * s_south(w) * w
    s_cz = VERTICAL * (w[:-2] * w[2:])
    nothing = jnp.zeros((2, 8, LANES), F32)
    s_d = 1.0 - (s_ce + s_cw) - (s_cn + s_cs)
    s_d = s_d - jnp.concatenate([s_cz, nothing], 0) - jnp.concatenate([nothing, s_cz], 0)
    for i, part in enumerate((s_d, s_ce, s_cw, s_cn, s_cs)):
        s_c[i] = part
    s_c[5, 0:10] = s_cz

    def by_tile(count, unroll, one):
        def several(i, carry):
            for q in range(unroll):
                r = i * unroll + q
                t = pl.multiple_of(8 * r, 8)
                one(r, t)
            return carry

        lax.fori_loop(0, count // unroll, several, 0)

    def coefficients(r, t):
        at = pl.ds(t + 8, 8)
        ce, cn = x_ref[COEF : COEF + 1, at], x_ref[COEF + 1 : COEF + 2, at]
        cs = x_ref[COEF + 1 : COEF + 2, pl.ds(t + 7, 8)]
        _, ce_west = beside(ce, *level(COEF), r)
        tiles = [x_ref[WET + k : WET + k + 1, at] for k in range(K)]
        below = None
        for k in range(K):
            wk = tiles[k]
            w_east, w_west = beside(wk, *level(WET + k), r)
            e, wst = ce * wk * w_east, ce_west * w_west * wk
            n = cn * wk * x_ref[WET + k : WET + k + 1, pl.ds(t + 9, 8)]
            s = cs * x_ref[WET + k : WET + k + 1, pl.ds(t + 7, 8)] * wk
            d = 1.0 - (e + wst) - (n + s)
            if k < K - 1:
                z = VERTICAL * (wk * tiles[k + 1])
                c_z[k : k + 1, pl.ds(t, 8)] = z
                d = d - z
            if below is not None:
                d = d - below
            below = z
            c_e[k : k + 1, pl.ds(t, 8)] = e
            c_w[k : k + 1, pl.ds(t, 8)] = wst
            c_n[k : k + 1, at] = n
            diag[k : k + 1, pl.ds(t, 8)] = d

    by_tile(TILES, COEF_UNROLL, coefficients)

    def strip_product(base):
        x = s_ref[pl.ds(2 * base, 2 * K)]
        out = s_c[0] * x + (s_c[1] * lane_roll(x, -1) + s_c[2] * lane_roll(x, 1))
        out = out + (s_c[3] * s_north(x) + s_c[4] * s_south(x))
        cz = s_c[5, 0:10]
        return out + jnp.concatenate([cz * x[2:], nothing], 0) + jnp.concatenate([nothing, cz * x[:-2]], 0)

    def product(base, r, t):
        here, at = pl.ds(t, 8), pl.ds(t + 8, 8)
        north, south = pl.ds(t + 9, 8), pl.ds(t + 7, 8)
        x = [x_ref[pl.ds(base + k, 1), at] for k in range(K)]
        out = []
        for k in range(K):
            one = pl.ds(base + k, 1)
            x_east, x_west = beside(x[k], s_ref[pl.ds(2 * (base + k), 1)], s_ref[pl.ds(2 * (base + k) + 1, 1)], r)
            p = diag[k : k + 1, here] * x[k]
            p = p + (c_e[k : k + 1, here] * x_east + c_w[k : k + 1, here] * x_west)
            p = p + (c_n[k : k + 1, at] * x_ref[one, north] + c_n[k : k + 1, south] * x_ref[one, south])
            if k < K - 1:
                p = p + c_z[k : k + 1, here] * x[k + 1]
            if k > 0:
                p = p + c_z[k - 1 : k, here] * x[k - 1]
            out.append(p)
        return out

    def forward(n, carry):
        now = OTHER * lax.rem(n, 2)
        later = OTHER - now
        bounded = jnp.tanh(strip_product(now))
        s_gain[n] = 1.0 - bounded * bounded
        s_ref[pl.ds(2 * later, 2 * K)] = bounded + s_ref[2 * SOURCE : 2 * SOURCE + 2 * K]

        def one(r, t):
            for k, p in enumerate(product(now, r, t)):
                bounded = jnp.tanh(p)
                gain[n, k : k + 1, pl.ds(t, 8)] = 1.0 - bounded * bounded
                at = pl.ds(t + 8, 8)
                x_ref[pl.ds(later + k, 1), at] = bounded + x_ref[SOURCE + k : SOURCE + k + 1, at]

        by_tile(TILES, UNROLL, one)
        return carry

    lax.fori_loop(0, STEPS, forward, 0)

    def turn(k, carry):
        one, o = pl.ds(k, 1), pl.ds(16, ROWS)
        final_ref[one] = x_ref[pl.ds(WET + k, 1), o] * x_ref[pl.ds(STATE + k, 1), o]
        x_ref[one, 8:72] = gain[STEPS - 1, one] * x_ref[pl.ds(COT + k, 1), 8:72]
        return carry

    lax.fori_loop(0, K, turn, 0)
    s_ref[0 : 2 * K] = s_gain[STEPS - 1] * s_ref[2 * COT : 2 * COT + 2 * K]

    def backward(m, carry):
        n = STEPS - 1 - m
        before = jnp.maximum(n - 1, 0)
        now = OTHER * lax.rem(m, 2)
        later = OTHER - now
        s_ref[pl.ds(2 * later, 2 * K)] = s_gain[before] * strip_product(now)

        def one(r, t):
            for k, p in enumerate(product(now, r, t)):
                here = pl.ds(t, 8)
                adj[n, k : k + 1, here] = p
                x_ref[pl.ds(later + k, 1), pl.ds(t + 8, 8)] = gain[before, k : k + 1, here] * p

        by_tile(TILES, UNROLL, one)
        return carry

    lax.fori_loop(0, STEPS, backward, 0)

    def finish(k, carry):
        one, o = pl.ds(k, 1), pl.ds(8, ROWS)
        wk = x_ref[pl.ds(WET + k, 1), 16 : 16 + ROWS]
        gini_ref[one] = wk * adj[0, one, o]
        gsrc_ref[one] = wk * (
            x_ref[pl.ds(COT + k, 1), 16 : 16 + ROWS] + adj[1, one, o] + (adj[2, one, o] + adj[3, one, o])
        )
        return carry

    lax.fori_loop(0, K, finish, 0)
    for copy in copies:
        copy.wait_send()


def store(a_ref, b_ref, c_ref, a_out, b_out, c_out, sem):
    copies = [
        pltpu.make_async_copy(src_ref, dst_ref, sem.at[i])
        for i, (src_ref, dst_ref) in enumerate(((a_ref, a_out), (b_ref, b_out), (c_ref, c_out)))
    ]
    for copy in copies:
        copy.start()
    for copy in copies:
        copy.wait()


def body(initial_state, source, cotangent, face_coefs, land_mask, bottom):
    out = pltpu.VMEM((K, ROWS, LANES), F32)
    tiles = pltpu.VMEM((K, 8 * TILES, LANES), F32)
    pairs = pltpu.VMEM((PAIRS, 8, LANES), F32)
    steps = pltpu.VMEM((STEPS, K, 8 * TILES, LANES), F32)
    corner = pltpu.VMEM((4, 2, 8, LANES), F32)
    results = pl.pallas_call(
        kernel,
        name="window",
        out_shape=(out, out, out),
        in_specs=[pl.BlockSpec(memory_space=pl.ANY)] * 6,
        out_specs=(pl.BlockSpec(memory_space=pltpu.VMEM),) * 3,
        scratch_shapes=[
            pltpu.VMEM((PLANES + K, PAD, LANES), F32),
            pltpu.VMEM((K, 8 * TILES, LANES), jnp.int32),
            pltpu.VMEM((8 * TILES, LANES), jnp.int32),
            tiles, tiles, pltpu.VMEM((K, PAD, LANES), F32), tiles, tiles,
            steps, steps,
            pltpu.VMEM((2 * PAIRS, 8, LANES), F32),
            pairs, pairs, corner, pairs, pairs, corner,
            pltpu.VMEM((2 * (PLANES + K), 8, LANES), F32),
            pltpu.VMEM((6, 2 * K, 8, LANES), F32),
            pltpu.VMEM((STEPS, 2 * K, 8, LANES), F32),
            pltpu.SemaphoreType.DMA((6,)),
            pltpu.SemaphoreType.DMA((18,)),
            pltpu.SemaphoreType.DMA((18,)),
        ],
        compiler_params=pltpu.CompilerParams(collective_id=0, has_side_effects=True),
    )(initial_state, source, cotangent, face_coefs, land_mask, bottom)
    plain = jax.ShapeDtypeStruct((K, ROWS, LANES), F32)
    return pl.pallas_call(
        store,
        name="store",
        out_shape=(plain,) * 3,
        in_specs=[pl.BlockSpec(memory_space=pltpu.VMEM)] * 3,
        out_specs=(pl.BlockSpec(memory_space=pl.ANY),) * 3,
        scratch_shapes=[pltpu.SemaphoreType.DMA((3,))],
    )(*[pltpu.with_memory_space_constraint(x, pltpu.VMEM) for x in results])


def solution(mesh):
    spec = P(None, "lat", "lon")
    return jax.shard_map(
        body,
        mesh=mesh,
        in_specs=(spec,) * 5 + (P("lat", "lon"),),
        out_specs=(spec,) * 3,
        check_vma=False,
    )
```

```python
import jax
import jax.numpy as jnp
from jax import lax
from jax.experimental import pallas as pl
from jax.experimental.pallas import tpu as pltpu
from jax.sharding import PartitionSpec as P

MESH = pl.DeviceIdType.MESH
STEPS = 4
K = 6
ROWS = 48
LANES = 128
TILES = 8
PAD = 80
GROUP = 7
COEF_UNROLL = 2
VERTICAL = 0.04
F32 = jnp.float32

STATE, WET, COEF, SOURCE, COT, OTHER = 0, 6, 12, 14, 20, 26
PLANES = 26
FRINGE = 4
PAIRS = PLANES // 2 + 1


def lane_roll(x, shift):
    if isinstance(shift, int):
        shift %= LANES
    return pltpu.roll(x, shift, x.ndim - 1)


def kernel(
    state_hbm, source_hbm, cot_hbm, coef_hbm, mask_hbm, bottom_hbm,
    final_ref, gini_ref, gsrc_ref,
    x_ref, mask, bottom,
    c_e, c_w, c_edge, c_n, c_z, diag, gain, adj,
    packed, pack_e, pack_w, corner_out, got_w, got_e, corner_in,
    s_ref, s_c, s_gain,
    load_sem, send_sem, recv_sem,
):
    lat, lon = lax.axis_index("lat"), lax.axis_index("lon")
    n_lat, n_lon = lax.axis_size("lat"), lax.axis_size("lon")
    up, down = lax.rem(lat + 1, n_lat), lax.rem(lat + n_lat - 1, n_lat)
    east, west = lax.rem(lon + 1, n_lon), lax.rem(lon + n_lon - 1, n_lon)
    has_up, has_down = lat < n_lat - 1, lat > 0

    barrier = pltpu.get_barrier_semaphore()

    def greet(devices):
        for device in devices:
            pl.semaphore_signal(barrier, inc=1, device_id=device, device_id_type=MESH)

    greet([(lat, east), (lat, west)])
    pl.when(has_up)(lambda: greet([(up, lon), (up, east), (up, west)]))
    pl.when(has_down)(lambda: greet([(down, lon), (down, east), (down, west)]))

    lane = lax.broadcasted_iota(jnp.int32, (1, 8, LANES), 2)
    sub = lax.broadcasted_iota(jnp.int32, (1, 8, LANES), 1)
    block = lane // 16
    left = lane % 16 < 8

    def planes(start, count):
        return x_ref.at[pl.ds(start, count)]

    fields = [
        (mask_hbm, mask, 8, 8),
        (bottom_hbm, bottom, 8, 8),
        (coef_hbm, planes(COEF, 2), 16, 8),
        (state_hbm, planes(STATE, K), 16, 8),
        (source_hbm, planes(SOURCE, K), 16, 8),
        (cot_hbm, planes(COT, K), 16, FRINGE),
    ]
    urgent, later_fields = range(4), range(4, 6)

    def rows_of(ref, start, size):
        if len(ref.shape) == 2:
            return ref.at[pl.ds(start, size)]
        return ref.at[:, pl.ds(start, size)]

    loads = [
        pltpu.make_async_copy(hbm, rows_of(ref, first, ROWS), load_sem.at[i])
        for i, (hbm, ref, first, _) in enumerate(fields)
    ]
    for load in loads:
        load.start()

    def remote(src_ref, dst_ref, i, device):
        return pltpu.make_async_remote_copy(
            src_ref=src_ref, dst_ref=dst_ref, send_sem=send_sem.at[i], recv_sem=recv_sem.at[i],
            device_id=device, device_id_type=MESH,
        )

    rows_up = [
        remote(rows_of(hbm, ROWS - size, size), rows_of(ref, first - size, size), i, (up, lon))
        for i, (hbm, ref, first, size) in enumerate(fields)
    ]
    rows_down = [
        remote(rows_of(hbm, 0, size), rows_of(ref, first + ROWS, size), 6 + i, (down, lon))
        for i, (hbm, ref, first, size) in enumerate(fields)
    ]

    def strip_copies(g):
        part = pl.ds(GROUP * g, GROUP)
        return [
            remote(pack_e.at[part], got_w.at[part], 12 + g, (lat, east)),
            remote(pack_w.at[part], got_e.at[part], 14 + g, (lat, west)),
        ]

    def corners_up(g):
        return [
            remote(corner_out.at[c, g], corner_in.at[c, g], 16 + 2 * c + g, (up, side))
            for c, side in ((0, east), (1, west))
        ]

    def corners_down(g):
        return [
            remote(corner_out.at[c, g], corner_in.at[c, g], 16 + 2 * c + g, (down, side))
            for c, side in ((2, east), (3, west))
        ]

    def start(copies):
        for copy in copies:
            copy.start()

    def received(copies):
        for copy in copies:
            copy.wait_recv()

    def sent(copies):
        for copy in copies:
            copy.wait_send()

    zero_tile = jnp.zeros((1, 8, LANES), F32)

    def clear(p, carry):
        x_ref[pl.ds(p, 1), 0:8] = zero_tile
        x_ref[pl.ds(p, 1), 72:80] = zero_tile
        return carry

    lax.fori_loop(0, PLANES + K, clear, 0)
    c_n[:, 0:8] = jnp.zeros((K, 8, LANES), F32)
    x_ref[COT : COT + K, 8 : 16 - FRINGE] = jnp.zeros((K, 8 - FRINGE, LANES), F32)
    x_ref[COT : COT + K, 64 + FRINGE : 72] = jnp.zeros((K, 8 - FRINGE, LANES), F32)

    def beyond_pole(rows, corner):
        x_ref[0:PLANES, rows : rows + 8] = jnp.zeros((PLANES, 8, LANES), F32)
        corner_in[corner : corner + 2] = jnp.zeros((2, 2, 8, LANES), F32)

    pl.when(jnp.logical_not(has_down))(lambda: beyond_pole(8, 0))
    pl.when(jnp.logical_not(has_up))(lambda: beyond_pole(64, 2))

    pl.semaphore_wait(barrier, 2 + 3 * (has_up.astype(jnp.int32) + has_down.astype(jnp.int32)))

    pl.when(has_up)(lambda: start([rows_up[i] for i in urgent]))
    pl.when(has_down)(lambda: start([rows_down[i] for i in urgent]))

    def wet_rows(first, size):
        for k in range(K):
            here = pl.ds(first, size)
            x_ref[WET + k, pl.ds(first + 8, size)] = jnp.where(k < bottom[here], mask[k, here], 0).astype(F32)

    def pack(g, j):
        i = GROUP * g + j
        both = []
        for q in range(2):
            total = zero_tile
            for t in range(6):
                moved = lane_roll(x_ref[pl.ds(2 * i + q, 1), 16 + 8 * t : 24 + 8 * t], 16 * (t + 1) + 8)
                total = moved if t == 0 else jnp.where(block == t + 1, moved, total)
            packed[pl.ds(2 * i + q, 1)] = total
            both.append(total)
        to_east = jnp.where(left, both[0], lane_roll(both[1], 8))
        to_west = jnp.where(left, lane_roll(both[0], -8), both[1])
        pack_e[pl.ds(i, 1)] = to_east
        pack_w[pl.ds(i, 1)] = to_west
        return [
            lane_roll(value, 16 * (j - source_block))
            for value, source_block in ((to_east, 6), (to_west, 6), (to_east, 1), (to_west, 1))
        ]

    def pack_group(g, carry):
        @pl.when(g == 0)
        def _():
            for i in urgent:
                loads[i].wait()
            wet_rows(8, ROWS)

        @pl.when(g == 1)
        def _():
            for i in later_fields:
                loads[i].wait()

        corner = [zero_tile] * 4
        for j in range(GROUP):
            corner = [jnp.where(block == j, new, old) for new, old in zip(pack(g, j), corner)]
        for c in range(4):
            corner_out[c, pl.ds(g, 1)] = corner[c]
        start(strip_copies(g))
        pl.when(has_up)(lambda: start(corners_up(g)))
        pl.when(has_down)(lambda: start(corners_down(g)))
        return carry

    lax.fori_loop(0, 2, pack_group, 0)
    pl.when(has_up)(lambda: start([rows_up[i] for i in later_fields]))
    pl.when(has_down)(lambda: start([rows_down[i] for i in later_fields]))

    def unpack(g, j):
        i = GROUP * g + j
        sides = []
        for ref, low, high in ((got_w, 0, 2), (got_e, 1, 3)):
            total = ref[pl.ds(i, 1)]
            total = jnp.where(block == 0, lane_roll(corner_in[low, pl.ds(g, 1)], -16 * j), total)
            total = jnp.where(block == 7, lane_roll(corner_in[high, pl.ds(g, 1)], 16 * (7 - j)), total)
            sides.append(total)
        from_west, from_east = sides
        for q in range(2):
            p = 2 * i + q
            mine = packed[pl.ds(p, 1)]
            mine = jnp.where(block == 0, lane_roll(x_ref[pl.ds(p, 1), 8:16], 8), mine)
            mine = jnp.where(block == 7, lane_roll(x_ref[pl.ds(p, 1), 64:72], 120), mine)
            a = from_west if q == 0 else lane_roll(from_west, -8)
            b = lane_roll(from_east, 8) if q == 0 else from_east
            s_ref[pl.ds(2 * p, 1)] = jnp.where(left, a, mine)
            s_ref[pl.ds(2 * p + 1, 1)] = jnp.where(left, mine, b)

    def s_north(x):
        rolled = pltpu.roll(x, 7, 1)
        return jnp.where(sub == 7, lane_roll(rolled, -16), rolled)

    def s_south(x):
        rolled = pltpu.roll(x, 1, 1)
        return jnp.where(sub == 0, lane_roll(rolled, 16), rolled)

    def beside(x, a, b, r):
        turned = lane_roll(jnp.where(left, a, b), lax.rem(120 + LANES - 16 * r, LANES))
        return (
            lane_roll(jnp.where(lane == 0, turned, x), -1),
            lane_roll(jnp.where(lane == LANES - 1, turned, x), 1),
        )

    def level(p):
        return s_ref[2 * p : 2 * p + 1], s_ref[2 * p + 1 : 2 * p + 2]

    def by_tile(count, unroll, one):
        def several(i, carry):
            for q in range(unroll):
                r = i * unroll + q
                one(r, pl.multiple_of(8 * r, 8))
            return carry

        lax.fori_loop(0, count // unroll, several, 0)

    nothing = jnp.zeros((2, 8, LANES), F32)

    def strip_coefficients():
        def six(pair):
            return jnp.concatenate([pair] * K, 0)

        w = s_ref[2 * WET : 2 * WET + 2 * K]
        all_e = six(s_ref[2 * COEF : 2 * COEF + 2])
        all_n = six(s_ref[2 * COEF + 2 : 2 * COEF + 4])
        s_ce = all_e * w * lane_roll(w, -1)
        s_cw = lane_roll(all_e, 1) * lane_roll(w, 1) * w
        s_cn = all_n * w * s_north(w)
        s_cs = s_south(all_n) * s_south(w) * w
        s_cz = VERTICAL * (w[:-2] * w[2:])
        s_d = 1.0 - (s_ce + s_cw) - (s_cn + s_cs)
        s_d = s_d - jnp.concatenate([s_cz, nothing], 0) - jnp.concatenate([nothing, s_cz], 0)
        for i, part in enumerate((s_d, s_ce, s_cw, s_cn, s_cs)):
            s_c[i] = part
        s_c[5, 0:10] = s_cz

    def coefficients(r, t):
        here, at = pl.ds(t, 8), pl.ds(t + 8, 8)
        ce, cn = x_ref[COEF : COEF + 1, at], x_ref[COEF + 1 : COEF + 2, at]
        cs = x_ref[COEF + 1 : COEF + 2, pl.ds(t + 7, 8)]
        _, ce_west = beside(ce, *level(COEF), r)
        tiles = [x_ref[WET + k : WET + k + 1, at] for k in range(K)]
        below = None
        for k in range(K):
            wk = tiles[k]
            w_east, w_west = beside(wk, *level(WET + k), r)
            e, wst = ce * wk * w_east, ce_west * w_west * wk
            n = cn * wk * x_ref[WET + k : WET + k + 1, pl.ds(t + 9, 8)]
            s = cs * x_ref[WET + k : WET + k + 1, pl.ds(t + 7, 8)] * wk
            d = 1.0 - (e + wst) - (n + s)
            if k < K - 1:
                z = VERTICAL * (wk * tiles[k + 1])
                c_z[k : k + 1, here] = z
                d = d - z
            if below is not None:
                d = d - below
            below = z
            first, last = lane == 0, lane == LANES - 1
            c_e[k : k + 1, here] = jnp.where(last, 0.0, e)
            c_w[k : k + 1, here] = jnp.where(first, 0.0, wst)
            c_edge[k : k + 1, here] = jnp.where(first, wst, jnp.where(last, e, 0.0))
            c_n[k : k + 1, at] = n
            diag[k : k + 1, here] = d

    def unpack_group(g, carry):
        @pl.when(g == 0)
        def _():
            pl.when(has_down)(lambda: received([rows_up[i] for i in urgent]))
            pl.when(has_up)(lambda: received([rows_down[i] for i in urgent]))
            pl.when(has_down)(lambda: wet_rows(0, 8))
            pl.when(has_up)(lambda: wet_rows(ROWS + 8, 8))

        @pl.when(g == 1)
        def _():
            pl.when(has_down)(lambda: received([rows_up[i] for i in later_fields]))
            pl.when(has_up)(lambda: received([rows_down[i] for i in later_fields]))

        received(strip_copies(g))
        pl.when(has_down)(lambda: received(corners_up(g)))
        pl.when(has_up)(lambda: received(corners_down(g)))
        for j in range(GROUP):
            unpack(g, j)

        @pl.when(g == 0)
        def _():
            strip_coefficients()
            by_tile(TILES, COEF_UNROLL, coefficients)

        return carry

    lax.fori_loop(0, 2, unpack_group, 0)

    def strip_product(base):
        x = s_ref[pl.ds(2 * base, 2 * K)]
        x_east, x_west = lane_roll(x, -1), lane_roll(x, 1)
        out = s_c[0] * x + (s_c[1] * x_east + s_c[2] * x_west)
        out = out + (s_c[3] * s_north(x) + s_c[4] * s_south(x))
        cz = s_c[5, 0:10]
        out = out + jnp.concatenate([cz * x[2:], nothing], 0) + jnp.concatenate([nothing, cz * x[:-2]], 0)
        return out, [jnp.where(left, x_east[2 * k + 1 : 2 * k + 2], x_west[2 * k : 2 * k + 1]) for k in range(K)]

    def product(base, edges, r, t):
        here, at = pl.ds(t, 8), pl.ds(t + 8, 8)
        north, south = pl.ds(t + 9, 8), pl.ds(t + 7, 8)
        x = [x_ref[pl.ds(base + k, 1), at] for k in range(K)]
        out = []
        for k in range(K):
            one = pl.ds(base + k, 1)
            edge = lane_roll(edges[k], 120 - 16 * r)
            p = c_e[k : k + 1, here] * lane_roll(x[k], -1) + c_w[k : k + 1, here] * lane_roll(x[k], 1)
            p = p + (c_edge[k : k + 1, here] * edge + diag[k : k + 1, here] * x[k])
            p = p + (c_n[k : k + 1, at] * x_ref[one, north] + c_n[k : k + 1, south] * x_ref[one, south])
            if k < K - 1:
                p = p + c_z[k : k + 1, here] * x[k + 1]
            if k > 0:
                p = p + c_z[k - 1 : k, here] * x[k - 1]
            out.append(p)
        return out

    def all_tiles(one):
        for r in range(TILES):
            one(r, 8 * r)

    def forward(n, carry):
        now = OTHER * lax.rem(n, 2)
        later = OTHER - now
        p, edges = strip_product(now)
        bounded = jnp.tanh(p)
        s_gain[n] = 1.0 - bounded * bounded
        s_ref[pl.ds(2 * later, 2 * K)] = bounded + s_ref[2 * SOURCE : 2 * SOURCE + 2 * K]

        def one(r, t):
            for k, p in enumerate(product(now, edges, r, t)):
                bounded = jnp.tanh(p)
                gain[n, k : k + 1, pl.ds(t, 8)] = 1.0 - bounded * bounded
                at = pl.ds(t + 8, 8)
                x_ref[pl.ds(later + k, 1), at] = bounded + x_ref[SOURCE + k : SOURCE + k + 1, at]

        all_tiles(one)
        return carry

    lax.fori_loop(0, STEPS, forward, 0)

    def turn(k, carry):
        one, o = pl.ds(k, 1), pl.ds(16, ROWS)
        final_ref[one] = x_ref[pl.ds(WET + k, 1), o] * x_ref[pl.ds(STATE + k, 1), o]
        x_ref[one, 8:72] = gain[STEPS - 1, one] * x_ref[pl.ds(COT + k, 1), 8:72]
        return carry

    lax.fori_loop(0, K, turn, 0)
    s_ref[0 : 2 * K] = s_gain[STEPS - 1] * s_ref[2 * COT : 2 * COT + 2 * K]

    def backward(m, carry):
        n = STEPS - 1 - m
        before = jnp.maximum(n - 1, 0)
        now = OTHER * lax.rem(m, 2)
        later = OTHER - now
        p, edges = strip_product(now)
        s_ref[pl.ds(2 * later, 2 * K)] = s_gain[before] * p

        def one(r, t):
            for k, p in enumerate(product(now, edges, r, t)):
                here = pl.ds(t, 8)
                adj[n, k : k + 1, here] = p
                x_ref[pl.ds(later + k, 1), pl.ds(t + 8, 8)] = gain[before, k : k + 1, here] * p

        all_tiles(one)
        return carry

    lax.fori_loop(0, STEPS, backward, 0)

    def finish(k, carry):
        one, o = pl.ds(k, 1), pl.ds(8, ROWS)
        wk = x_ref[pl.ds(WET + k, 1), 16 : 16 + ROWS]
        gini_ref[one] = wk * adj[0, one, o]
        gsrc_ref[one] = wk * (
            x_ref[pl.ds(COT + k, 1), 16 : 16 + ROWS] + adj[1, one, o] + (adj[2, one, o] + adj[3, one, o])
        )
        return carry

    lax.fori_loop(0, K, finish, 0)
    pl.when(has_up)(lambda: sent(rows_up))
    pl.when(has_down)(lambda: sent(rows_down))
    for g in range(2):
        sent(strip_copies(g))
        pl.when(has_up)(lambda: sent(corners_up(g)))
        pl.when(has_down)(lambda: sent(corners_down(g)))


def store(a_ref, b_ref, c_ref, a_out, b_out, c_out, sem):
    copies = [
        pltpu.make_async_copy(src_ref, dst_ref, sem.at[i])
        for i, (src_ref, dst_ref) in enumerate(((a_ref, a_out), (b_ref, b_out), (c_ref, c_out)))
    ]
    for copy in copies:
        copy.start()
    for copy in copies:
        copy.wait()


def body(initial_state, source, cotangent, face_coefs, land_mask, bottom):
    out = pltpu.VMEM((K, ROWS, LANES), F32)
    tiles = pltpu.VMEM((K, 8 * TILES, LANES), F32)
    pairs = pltpu.VMEM((PAIRS, 8, LANES), F32)
    steps = pltpu.VMEM((STEPS, K, 8 * TILES, LANES), F32)
    corner = pltpu.VMEM((4, 2, 8, LANES), F32)
    results = pl.pallas_call(
        kernel,
        name="window",
        out_shape=(out, out, out),
        in_specs=[pl.BlockSpec(memory_space=pl.ANY)] * 6,
        out_specs=(pl.BlockSpec(memory_space=pltpu.VMEM),) * 3,
        scratch_shapes=[
            pltpu.VMEM((PLANES + K, PAD, LANES), F32),
            pltpu.VMEM((K, 8 * TILES, LANES), jnp.int32),
            pltpu.VMEM((8 * TILES, LANES), jnp.int32),
            tiles, tiles, tiles, pltpu.VMEM((K, PAD, LANES), F32), tiles, tiles,
            steps, steps,
            pltpu.VMEM((2 * PAIRS, 8, LANES), F32),
            pairs, pairs, corner, pairs, pairs, corner,
            pltpu.VMEM((2 * (PLANES + K), 8, LANES), F32),
            pltpu.VMEM((6, 2 * K, 8, LANES), F32),
            pltpu.VMEM((STEPS, 2 * K, 8, LANES), F32),
            pltpu.SemaphoreType.DMA((6,)),
            pltpu.SemaphoreType.DMA((24,)),
            pltpu.SemaphoreType.DMA((24,)),
        ],
        compiler_params=pltpu.CompilerParams(collective_id=0, has_side_effects=True),
    )(initial_state, source, cotangent, face_coefs, land_mask, bottom)
    plain = jax.ShapeDtypeStruct((K, ROWS, LANES), F32)
    return pl.pallas_call(
        store,
        name="store",
        out_shape=(plain,) * 3,
        in_specs=[pl.BlockSpec(memory_space=pltpu.VMEM)] * 3,
        out_specs=(pl.BlockSpec(memory_space=pl.ANY),) * 3,
        scratch_shapes=[pltpu.SemaphoreType.DMA((3,))],
    )(*[pltpu.with_memory_space_constraint(x, pltpu.VMEM) for x in results])


def solution(mesh):
    spec = P(None, "lat", "lon")
    return jax.shard_map(
        body,
        mesh=mesh,
        in_specs=(spec,) * 5 + (P("lat", "lon"),),
        out_specs=(spec,) * 3,
        check_vma=False,
    )
```

```python
import jax
import jax.numpy as jnp
from jax import lax
from jax.experimental import pallas as pl
from jax.experimental.pallas import tpu as pltpu
from jax.sharding import PartitionSpec as P

MESH = pl.DeviceIdType.MESH
STEPS = 4
K = 6
ROWS = 48
LANES = 128
TILES = 8
PAD = 80
GROUP = 7
VERTICAL = 0.04
F32 = jnp.float32

STATE, WET, COEF, SOURCE, COT, OTHER = 0, 6, 12, 14, 20, 26
PLANES = 26
FRINGE = 4
PAIRS = PLANES // 2 + 1


def lane_roll(x, shift):
    if isinstance(shift, int):
        shift %= LANES
    return pltpu.roll(x, shift, x.ndim - 1)


def kernel(
    state_hbm, source_hbm, cot_hbm, coef_hbm, mask_hbm, bottom_hbm,
    final_ref, gini_ref, gsrc_ref,
    x_ref, mask, bottom,
    c_e, c_w, c_edge, c_n, c_z, diag, gain, adj,
    packed, pack_e, pack_w, corner_out, got_w, got_e, corner_in,
    s_ref, s_c, s_gain,
    load_sem, send_sem, recv_sem,
):
    lat, lon = lax.axis_index("lat"), lax.axis_index("lon")
    n_lat, n_lon = lax.axis_size("lat"), lax.axis_size("lon")
    up, down = lax.rem(lat + 1, n_lat), lax.rem(lat + n_lat - 1, n_lat)
    east, west = lax.rem(lon + 1, n_lon), lax.rem(lon + n_lon - 1, n_lon)
    has_up, has_down = lat < n_lat - 1, lat > 0

    barrier = pltpu.get_barrier_semaphore()

    def greet(devices):
        for device in devices:
            pl.semaphore_signal(barrier, inc=1, device_id=device, device_id_type=MESH)

    greet([(lat, east), (lat, west)])
    pl.when(has_up)(lambda: greet([(up, lon), (up, east), (up, west)]))
    pl.when(has_down)(lambda: greet([(down, lon), (down, east), (down, west)]))

    lane = lax.broadcasted_iota(jnp.int32, (1, 8, LANES), 2)
    sub = lax.broadcasted_iota(jnp.int32, (1, 8, LANES), 1)
    block = lane // 16
    left = lane % 16 < 8

    def planes(start, count):
        return x_ref.at[pl.ds(start, count)]

    def rows_of(ref, start, size):
        return ref.at[:, pl.ds(start, size)]

    own = pl.ds(16, ROWS)
    loads = [
        pltpu.make_async_copy(hbm, ref, load_sem.at[i])
        for i, (hbm, ref) in enumerate(
            [
                (bottom_hbm, bottom),
                (mask_hbm, mask),
                (coef_hbm, x_ref.at[COEF : COEF + 2, own]),
                (state_hbm, x_ref.at[STATE : STATE + K, own]),
                (source_hbm, x_ref.at[SOURCE : SOURCE + K, own]),
                (cot_hbm, x_ref.at[COT : COT + K, own]),
            ]
        )
    ]
    for load in loads:
        load.start()

    def remote(src_ref, dst_ref, i, device):
        return pltpu.make_async_remote_copy(
            src_ref=src_ref, dst_ref=dst_ref, send_sem=send_sem.at[i], recv_sem=recv_sem.at[i],
            device_id=device, device_id_type=MESH,
        )

    parts = [(planes(0, SOURCE), 8), (planes(SOURCE, K), 8), (planes(COT, K), FRINGE)]
    rows_up = [
        remote(rows_of(ref, 64 - size, size), rows_of(ref, 16 - size, size), i, (up, lon))
        for i, (ref, size) in enumerate(parts)
    ]
    rows_down = [
        remote(rows_of(ref, 16, size), rows_of(ref, 64, size), 3 + i, (down, lon)) for i, (ref, size) in enumerate(parts)
    ]

    def strip_copies(g):
        part = pl.ds(GROUP * g, GROUP)
        return [
            remote(pack_e.at[part], got_w.at[part], 6 + g, (lat, east)),
            remote(pack_w.at[part], got_e.at[part], 8 + g, (lat, west)),
        ]

    def corners_up(g):
        return [
            remote(corner_out.at[c, g], corner_in.at[c, g], 10 + 2 * c + g, (up, side))
            for c, side in ((0, east), (1, west))
        ]

    def corners_down(g):
        return [
            remote(corner_out.at[c, g], corner_in.at[c, g], 10 + 2 * c + g, (down, side))
            for c, side in ((2, east), (3, west))
        ]

    def start(copies):
        for copy in copies:
            copy.start()

    def received(copies):
        for copy in copies:
            copy.wait_recv()

    def sent(copies):
        for copy in copies:
            copy.wait_send()

    zero_tile = jnp.zeros((1, 8, LANES), F32)

    def wet_cells():
        for k in range(K):
            x_ref[WET + k, own] = jnp.where(k < bottom[...], mask[k], 0).astype(F32)

    def pack(g, j):
        i = GROUP * g + j
        both = []
        for q in range(2):
            total = zero_tile
            for t in range(6):
                moved = lane_roll(x_ref[pl.ds(2 * i + q, 1), 16 + 8 * t : 24 + 8 * t], 16 * (t + 1) + 8)
                total = moved if t == 0 else jnp.where(block == t + 1, moved, total)
            packed[pl.ds(2 * i + q, 1)] = total
            both.append(total)
        to_east = jnp.where(left, both[0], lane_roll(both[1], 8))
        to_west = jnp.where(left, lane_roll(both[0], -8), both[1])
        pack_e[pl.ds(i, 1)] = to_east
        pack_w[pl.ds(i, 1)] = to_west
        return [
            lane_roll(value, 16 * (j - source_block))
            for value, source_block in ((to_east, 6), (to_west, 6), (to_east, 1), (to_west, 1))
        ]

    def pack_group(g, carry):
        @pl.when(g == 0)
        def _():
            for i in range(4):
                loads[i].wait()
            wet_cells()

        @pl.when(g == 1)
        def _():
            for i in range(4, 6):
                loads[i].wait()

        corner = [zero_tile] * 4
        for j in range(GROUP):
            corner = [jnp.where(block == j, new, old) for new, old in zip(pack(g, j), corner)]
        for c in range(4):
            corner_out[c, pl.ds(g, 1)] = corner[c]
        return carry

    lax.fori_loop(0, 2, pack_group, 0)
    pl.semaphore_wait(barrier, 2 + 3 * (has_up.astype(jnp.int32) + has_down.astype(jnp.int32)))

    def send_group(g, up_rows, down_rows):
        pl.when(has_up)(lambda: start(corners_up(g)))
        pl.when(has_down)(lambda: start(corners_down(g)))
        start(strip_copies(g))
        pl.when(has_up)(lambda: start(up_rows))
        pl.when(has_down)(lambda: start(down_rows))

    send_group(0, rows_up[:1], rows_down[:1])
    send_group(1, rows_up[1:], rows_down[1:])

    def clear(p, carry):
        x_ref[pl.ds(p, 1), 0:8] = zero_tile
        x_ref[pl.ds(p, 1), 72:80] = zero_tile
        return carry

    lax.fori_loop(0, PLANES + K, clear, 0)
    c_n[:, 0:8] = jnp.zeros((K, 8, LANES), F32)
    x_ref[COT : COT + K, 8 : 16 - FRINGE] = jnp.zeros((K, 8 - FRINGE, LANES), F32)
    x_ref[COT : COT + K, 64 + FRINGE : 72] = jnp.zeros((K, 8 - FRINGE, LANES), F32)

    def beyond_pole(rows, corner):
        x_ref[0:PLANES, rows : rows + 8] = jnp.zeros((PLANES, 8, LANES), F32)
        corner_in[corner : corner + 2] = jnp.zeros((2, 2, 8, LANES), F32)

    pl.when(jnp.logical_not(has_down))(lambda: beyond_pole(8, 0))
    pl.when(jnp.logical_not(has_up))(lambda: beyond_pole(64, 2))

    def unpack(g, j):
        i = GROUP * g + j
        sides = []
        for ref, low, high in ((got_w, 0, 2), (got_e, 1, 3)):
            total = ref[pl.ds(i, 1)]
            total = jnp.where(block == 0, lane_roll(corner_in[low, pl.ds(g, 1)], -16 * j), total)
            total = jnp.where(block == 7, lane_roll(corner_in[high, pl.ds(g, 1)], 16 * (7 - j)), total)
            sides.append(total)
        from_west, from_east = sides
        for q in range(2):
            p = 2 * i + q
            mine = packed[pl.ds(p, 1)]
            mine = jnp.where(block == 0, lane_roll(x_ref[pl.ds(p, 1), 8:16], 8), mine)
            mine = jnp.where(block == 7, lane_roll(x_ref[pl.ds(p, 1), 64:72], 120), mine)
            a = from_west if q == 0 else lane_roll(from_west, -8)
            b = lane_roll(from_east, 8) if q == 0 else from_east
            s_ref[pl.ds(2 * p, 1)] = jnp.where(left, a, mine)
            s_ref[pl.ds(2 * p + 1, 1)] = jnp.where(left, mine, b)

    def s_north(x):
        rolled = pltpu.roll(x, 7, 1)
        return jnp.where(sub == 7, lane_roll(rolled, -16), rolled)

    def s_south(x):
        rolled = pltpu.roll(x, 1, 1)
        return jnp.where(sub == 0, lane_roll(rolled, 16), rolled)

    nothing = jnp.zeros((2, 8, LANES), F32)

    def strip_coefficients():
        def six(pair):
            return jnp.concatenate([pair] * K, 0)

        w = s_ref[2 * WET : 2 * WET + 2 * K]
        all_e = six(s_ref[2 * COEF : 2 * COEF + 2])
        all_n = six(s_ref[2 * COEF + 2 : 2 * COEF + 4])
        s_ce = all_e * w * lane_roll(w, -1)
        s_cw = lane_roll(all_e, 1) * lane_roll(w, 1) * w
        s_cn = all_n * w * s_north(w)
        s_cs = s_south(all_n) * s_south(w) * w
        s_cz = VERTICAL * (w[:-2] * w[2:])
        s_d = 1.0 - (s_ce + s_cw) - (s_cn + s_cs)
        s_d = s_d - jnp.concatenate([s_cz, nothing], 0) - jnp.concatenate([nothing, s_cz], 0)
        for i, part in enumerate((s_d, s_ce, s_cw, s_cn, s_cs)):
            s_c[i] = part
        s_c[5, 0:10] = s_cz

    def coefficients(r):
        t = pl.multiple_of(8 * r, 8)
        here, at = pl.ds(t, 8), pl.ds(t + 8, 8)
        ce, cn = x_ref[COEF : COEF + 1, at], x_ref[COEF + 1 : COEF + 2, at]
        cs = x_ref[COEF + 1 : COEF + 2, pl.ds(t + 7, 8)]
        ce = jnp.where(lane == LANES - 1, 0.0, ce)
        tiles = [x_ref[WET + k : WET + k + 1, at] for k in range(K)]
        below = None
        for k in range(K):
            wk = tiles[k]
            e = ce * (wk * lane_roll(wk, -1))
            wst = lane_roll(e, 1)
            n = cn * wk * x_ref[WET + k : WET + k + 1, pl.ds(t + 9, 8)]
            s = cs * x_ref[WET + k : WET + k + 1, pl.ds(t + 7, 8)] * wk
            d = 1.0 - (e + wst) - (n + s)
            if k < K - 1:
                z = VERTICAL * (wk * tiles[k + 1])
                c_z[k : k + 1, here] = z
                d = d - z
            if below is not None:
                d = d - below
            below = z
            c_e[k : k + 1, here] = e
            c_w[k : k + 1, here] = wst
            c_n[k : k + 1, at] = n
            diag[k : k + 1, here] = d

    edge_lane = jnp.logical_or(lane == 0, lane == LANES - 1)

    def edge_coefficients(k, carry):
        one = pl.ds(k, 1)
        faces = jnp.where(left, s_c[1, pl.ds(2 * k + 1, 1)], s_c[2, pl.ds(2 * k, 1)])
        for r in range(TILES):
            here = pl.ds(8 * r, 8)
            c = jnp.where(edge_lane, lane_roll(faces, 120 - 16 * r), 0.0)
            c_edge[one, here] = c
            diag[one, here] = diag[one, here] - c
        return carry

    def unpack_group(g, carry):
        received(strip_copies(g))
        pl.when(has_down)(lambda: received(corners_up(g)))
        pl.when(has_up)(lambda: received(corners_down(g)))
        for j in range(GROUP):
            unpack(g, j)
        return carry

    def coefficient_group(i, carry):
        @pl.when(i == 2)
        def _():
            pl.when(has_down)(lambda: received(rows_up[:1]))
            pl.when(has_up)(lambda: received(rows_down[:1]))

        pair = lax.rem(i + 1, 3) + 2 * (i // 3)
        for q in range(2):
            coefficients(2 * pair + q)
        return carry

    lax.fori_loop(0, 4, coefficient_group, 0)

    def finish_group(g, carry):
        @pl.when(g == 1)
        def _():
            strip_coefficients()
            lax.fori_loop(0, K, edge_coefficients, 0)
            pl.when(has_down)(lambda: received(rows_up[1:]))
            pl.when(has_up)(lambda: received(rows_down[1:]))

        return unpack_group(g, carry)

    lax.fori_loop(0, 2, finish_group, 0)

    pl.when(has_up)(lambda: sent(rows_up[:1]))
    pl.when(has_down)(lambda: sent(rows_down[:1]))

    def strip_product(base):
        x = s_ref[pl.ds(2 * base, 2 * K)]
        x_east, x_west = lane_roll(x, -1), lane_roll(x, 1)
        out = s_c[0] * x + (s_c[1] * x_east + s_c[2] * x_west)
        out = out + (s_c[3] * s_north(x) + s_c[4] * s_south(x))
        cz = s_c[5, 0:10]
        out = out + jnp.concatenate([cz * x[2:], nothing], 0) + jnp.concatenate([nothing, cz * x[:-2]], 0)
        return out, [jnp.where(left, x_east[2 * k + 1 : 2 * k + 2], x_west[2 * k : 2 * k + 1]) for k in range(K)]

    def product(base, edges, r, t):
        here, at = pl.ds(t, 8), pl.ds(t + 8, 8)
        north, south = pl.ds(t + 9, 8), pl.ds(t + 7, 8)
        x = [x_ref[pl.ds(base + k, 1), at] for k in range(K)]
        out = []
        for k in range(K):
            one = pl.ds(base + k, 1)
            edge = lane_roll(edges[k], 120 - 16 * r)
            p = c_e[k : k + 1, here] * lane_roll(x[k], -1) + c_w[k : k + 1, here] * lane_roll(x[k], 1)
            p = p + (c_edge[k : k + 1, here] * edge + diag[k : k + 1, here] * x[k])
            p = p + (c_n[k : k + 1, at] * x_ref[one, north] + c_n[k : k + 1, south] * x_ref[one, south])
            if k < K - 1:
                p = p + c_z[k : k + 1, here] * x[k + 1]
            if k > 0:
                p = p + c_z[k - 1 : k, here] * x[k - 1]
            out.append(p)
        return out

    def all_tiles(one):
        for r in range(TILES):
            one(r, 8 * r)

    def forward(n, carry):
        now = OTHER * lax.rem(n, 2)
        later = OTHER - now
        p, edges = strip_product(now)
        bounded = jnp.tanh(p)
        s_gain[n] = 1.0 - bounded * bounded
        s_ref[pl.ds(2 * later, 2 * K)] = bounded + s_ref[2 * SOURCE : 2 * SOURCE + 2 * K]

        def one(r, t):
            for k, p in enumerate(product(now, edges, r, t)):
                bounded = jnp.tanh(p)
                gain[n, k : k + 1, pl.ds(t, 8)] = 1.0 - bounded * bounded
                at = pl.ds(t + 8, 8)
                x_ref[pl.ds(later + k, 1), at] = bounded + x_ref[SOURCE + k : SOURCE + k + 1, at]

        all_tiles(one)
        return carry

    lax.fori_loop(0, STEPS, forward, 0)

    def turn(k, carry):
        one, o = pl.ds(k, 1), pl.ds(16, ROWS)
        final_ref[one] = x_ref[pl.ds(WET + k, 1), o] * x_ref[pl.ds(STATE + k, 1), o]
        x_ref[one, 8:72] = gain[STEPS - 1, one] * x_ref[pl.ds(COT + k, 1), 8:72]
        return carry

    lax.fori_loop(0, K, turn, 0)
    s_ref[0 : 2 * K] = s_gain[STEPS - 1] * s_ref[2 * COT : 2 * COT + 2 * K]

    def backward(m, carry):
        n = STEPS - 1 - m
        before = jnp.maximum(n - 1, 0)
        now = OTHER * lax.rem(m, 2)
        later = OTHER - now
        p, edges = strip_product(now)
        s_ref[pl.ds(2 * later, 2 * K)] = s_gain[before] * p

        def one(r, t):
            for k, p in enumerate(product(now, edges, r, t)):
                here = pl.ds(t, 8)
                adj[n, k : k + 1, here] = p
                x_ref[pl.ds(later + k, 1), pl.ds(t + 8, 8)] = gain[before, k : k + 1, here] * p

        all_tiles(one)
        return carry

    lax.fori_loop(0, STEPS, backward, 0)

    def finish(k, carry):
        one, o = pl.ds(k, 1), pl.ds(8, ROWS)
        wk = x_ref[pl.ds(WET + k, 1), 16 : 16 + ROWS]
        gini_ref[one] = wk * adj[0, one, o]
        gsrc_ref[one] = wk * (
            x_ref[pl.ds(COT + k, 1), 16 : 16 + ROWS] + adj[1, one, o] + (adj[2, one, o] + adj[3, one, o])
        )
        return carry

    lax.fori_loop(0, K, finish, 0)
    pl.when(has_up)(lambda: sent(rows_up[1:]))
    pl.when(has_down)(lambda: sent(rows_down[1:]))
    for g in range(2):
        sent(strip_copies(g))
        pl.when(has_up)(lambda: sent(corners_up(g)))
        pl.when(has_down)(lambda: sent(corners_down(g)))


def store(a_ref, b_ref, c_ref, a_out, b_out, c_out, sem):
    copies = [
        pltpu.make_async_copy(src_ref, dst_ref, sem.at[i])
        for i, (src_ref, dst_ref) in enumerate(((a_ref, a_out), (b_ref, b_out), (c_ref, c_out)))
    ]
    for copy in copies:
        copy.start()
    for copy in copies:
        copy.wait()


def body(initial_state, source, cotangent, face_coefs, land_mask, bottom):
    out = pltpu.VMEM((K, ROWS, LANES), F32)
    tiles = pltpu.VMEM((K, 8 * TILES, LANES), F32)
    pairs = pltpu.VMEM((PAIRS, 8, LANES), F32)
    steps = pltpu.VMEM((STEPS, K, 8 * TILES, LANES), F32)
    corner = pltpu.VMEM((4, 2, 8, LANES), F32)
    results = pl.pallas_call(
        kernel,
        name="window",
        out_shape=(out, out, out),
        in_specs=[pl.BlockSpec(memory_space=pl.ANY)] * 6,
        out_specs=(pl.BlockSpec(memory_space=pltpu.VMEM),) * 3,
        scratch_shapes=[
            pltpu.VMEM((PLANES + K, PAD, LANES), F32),
            pltpu.VMEM((K, ROWS, LANES), jnp.int32),
            pltpu.VMEM((ROWS, LANES), jnp.int32),
            tiles, tiles, tiles, pltpu.VMEM((K, PAD, LANES), F32), tiles, tiles,
            steps, steps,
            pltpu.VMEM((2 * PAIRS, 8, LANES), F32),
            pairs, pairs, corner, pairs, pairs, corner,
            pltpu.VMEM((2 * (PLANES + K), 8, LANES), F32),
            pltpu.VMEM((6, 2 * K, 8, LANES), F32),
            pltpu.VMEM((STEPS, 2 * K, 8, LANES), F32),
            pltpu.SemaphoreType.DMA((6,)),
            pltpu.SemaphoreType.DMA((18,)),
            pltpu.SemaphoreType.DMA((18,)),
        ],
        compiler_params=pltpu.CompilerParams(collective_id=0, has_side_effects=True),
    )(initial_state, source, cotangent, face_coefs, land_mask, bottom)
    plain = jax.ShapeDtypeStruct((K, ROWS, LANES), F32)
    return pl.pallas_call(
        store,
        name="store",
        out_shape=(plain,) * 3,
        in_specs=[pl.BlockSpec(memory_space=pltpu.VMEM)] * 3,
        out_specs=(pl.BlockSpec(memory_space=pl.ANY),) * 3,
        scratch_shapes=[pltpu.SemaphoreType.DMA((3,))],
    )(*[pltpu.with_memory_space_constraint(x, pltpu.VMEM) for x in results])


def solution(mesh):
    spec = P(None, "lat", "lon")
    return jax.shard_map(
        body,
        mesh=mesh,
        in_specs=(spec,) * 5 + (P("lat", "lon"),),
        out_specs=(spec,) * 3,
        check_vma=False,
    )
```

```python
import jax
import jax.numpy as jnp
from jax import lax
from jax.experimental import pallas as pl
from jax.experimental.pallas import tpu as pltpu
from jax.sharding import PartitionSpec as P

MESH = pl.DeviceIdType.MESH
STEPS = 4
K = 6
ROWS = 48
LANES = 128
TILES = 8
PAD = 80
GROUP = 7
VERTICAL = 0.04
F32 = jnp.float32

STATE, WET, COEF, SOURCE, COT, OTHER = 0, 6, 12, 14, 20, 26
PLANES = 26
FRINGE = 4
PAIRS = PLANES // 2 + 1


def lane_roll(x, shift):
    if isinstance(shift, int):
        shift %= LANES
    return pltpu.roll(x, shift, x.ndim - 1)


def kernel(
    state_hbm, source_hbm, cot_hbm, coef_hbm, mask_hbm, bottom_hbm,
    final_ref, gini_ref, gsrc_ref,
    x_ref, mask, bottom,
    c_e, c_w, c_edge, c_n, c_z, diag, gain, adj,
    packed, pack_e, pack_w, corner_out, got_w, got_e, corner_in,
    s_ref, s_c, s_gain,
    load_sem, send_sem, recv_sem,
):
    lat, lon = lax.axis_index("lat"), lax.axis_index("lon")
    n_lat, n_lon = lax.axis_size("lat"), lax.axis_size("lon")
    up, down = lax.rem(lat + 1, n_lat), lax.rem(lat + n_lat - 1, n_lat)
    east, west = lax.rem(lon + 1, n_lon), lax.rem(lon + n_lon - 1, n_lon)
    has_up, has_down = lat < n_lat - 1, lat > 0

    barrier = pltpu.get_barrier_semaphore()

    def greet(devices):
        for device in devices:
            pl.semaphore_signal(barrier, inc=1, device_id=device, device_id_type=MESH)

    greet([(lat, east), (lat, west)])
    pl.when(has_up)(lambda: greet([(up, lon), (up, east), (up, west)]))
    pl.when(has_down)(lambda: greet([(down, lon), (down, east), (down, west)]))

    lane = lax.broadcasted_iota(jnp.int32, (1, 8, LANES), 2)
    sub = lax.broadcasted_iota(jnp.int32, (1, 8, LANES), 1)
    block = lane // 16
    left = lane % 16 < 8

    def planes(start, count):
        return x_ref.at[pl.ds(start, count)]

    def rows_of(ref, start, size):
        return ref.at[:, pl.ds(start, size)]

    own = pl.ds(16, ROWS)
    loads = [
        pltpu.make_async_copy(hbm, ref, load_sem.at[i])
        for i, (hbm, ref) in enumerate(
            [
                (bottom_hbm, bottom),
                (mask_hbm, mask),
                (coef_hbm, x_ref.at[COEF : COEF + 2, own]),
                (state_hbm, x_ref.at[STATE : STATE + K, own]),
                (source_hbm, x_ref.at[SOURCE : SOURCE + K, own]),
                (cot_hbm, x_ref.at[COT : COT + K, own]),
            ]
        )
    ]
    for load in loads:
        load.start()

    def remote(src_ref, dst_ref, i, device):
        return pltpu.make_async_remote_copy(
            src_ref=src_ref, dst_ref=dst_ref, send_sem=send_sem.at[i], recv_sem=recv_sem.at[i],
            device_id=device, device_id_type=MESH,
        )

    parts = [(planes(0, SOURCE), 8), (planes(SOURCE, K), 7), (planes(COT, K), FRINGE)]
    rows_up = [
        remote(rows_of(ref, 64 - size, size), rows_of(ref, 16 - size, size), i, (up, lon))
        for i, (ref, size) in enumerate(parts)
    ]
    rows_down = [
        remote(rows_of(ref, 16, size), rows_of(ref, 64, size), 3 + i, (down, lon)) for i, (ref, size) in enumerate(parts)
    ]

    def strip_copies(g):
        part = pl.ds(GROUP * g, GROUP)
        return [
            remote(pack_e.at[part], got_w.at[part], 6 + g, (lat, east)),
            remote(pack_w.at[part], got_e.at[part], 8 + g, (lat, west)),
        ]

    def corners_up(g):
        return [
            remote(corner_out.at[c, g], corner_in.at[c, g], 10 + 2 * c + g, (up, side))
            for c, side in ((0, east), (1, west))
        ]

    def corners_down(g):
        return [
            remote(corner_out.at[c, g], corner_in.at[c, g], 10 + 2 * c + g, (down, side))
            for c, side in ((2, east), (3, west))
        ]

    def start(copies):
        for copy in copies:
            copy.start()

    def received(copies):
        for copy in copies:
            copy.wait_recv()

    def sent(copies):
        for copy in copies:
            copy.wait_send()

    zero_tile = jnp.zeros((1, 8, LANES), F32)

    def wet_cells():
        for k in range(K):
            x_ref[WET + k, own] = jnp.where(k < bottom[...], mask[k], 0).astype(F32)

    def pack(g, j):
        i = GROUP * g + j
        both = []
        for q in range(2):
            total = zero_tile
            for t in range(6):
                moved = lane_roll(x_ref[pl.ds(2 * i + q, 1), 16 + 8 * t : 24 + 8 * t], 16 * (t + 1) + 8)
                total = moved if t == 0 else jnp.where(block == t + 1, moved, total)
            packed[pl.ds(2 * i + q, 1)] = total
            both.append(total)
        to_east = jnp.where(left, both[0], lane_roll(both[1], 8))
        to_west = jnp.where(left, lane_roll(both[0], -8), both[1])
        pack_e[pl.ds(i, 1)] = to_east
        pack_w[pl.ds(i, 1)] = to_west
        return [
            lane_roll(value, 16 * (j - source_block))
            for value, source_block in ((to_east, 6), (to_west, 6), (to_east, 1), (to_west, 1))
        ]

    def pack_group(g, carry):
        @pl.when(g == 0)
        def _():
            for i in range(4):
                loads[i].wait()
            wet_cells()

        @pl.when(g == 1)
        def _():
            for i in range(4, 6):
                loads[i].wait()

        corner = [zero_tile] * 4
        for j in range(GROUP):
            corner = [jnp.where(block == j, new, old) for new, old in zip(pack(g, j), corner)]
        for c in range(4):
            corner_out[c, pl.ds(g, 1)] = corner[c]
        return carry

    lax.fori_loop(0, 2, pack_group, 0)
    pl.semaphore_wait(barrier, 2 + 3 * (has_up.astype(jnp.int32) + has_down.astype(jnp.int32)))

    def send_group(g, up_rows, down_rows):
        pl.when(has_up)(lambda: start(corners_up(g)))
        pl.when(has_down)(lambda: start(corners_down(g)))
        start(strip_copies(g))
        pl.when(has_up)(lambda: start(up_rows))
        pl.when(has_down)(lambda: start(down_rows))

    send_group(0, rows_up[:1], rows_down[:1])
    send_group(1, rows_up[1:], rows_down[1:])

    def clear(p, carry):
        x_ref[pl.ds(p, 1), 0:8] = zero_tile
        x_ref[pl.ds(p, 1), 72:80] = zero_tile
        return carry

    lax.fori_loop(0, PLANES + K, clear, 0)
    c_n[:, 0:8] = jnp.zeros((K, 8, LANES), F32)
    x_ref[SOURCE : SOURCE + K, 8:9] = jnp.zeros((K, 1, LANES), F32)
    x_ref[SOURCE : SOURCE + K, 71:72] = jnp.zeros((K, 1, LANES), F32)
    x_ref[COT : COT + K, 8 : 16 - FRINGE] = jnp.zeros((K, 8 - FRINGE, LANES), F32)
    x_ref[COT : COT + K, 64 + FRINGE : 72] = jnp.zeros((K, 8 - FRINGE, LANES), F32)

    def beyond_pole(rows, corner):
        x_ref[0:PLANES, rows : rows + 8] = jnp.zeros((PLANES, 8, LANES), F32)
        corner_in[corner : corner + 2] = jnp.zeros((2, 2, 8, LANES), F32)

    pl.when(jnp.logical_not(has_down))(lambda: beyond_pole(8, 0))
    pl.when(jnp.logical_not(has_up))(lambda: beyond_pole(64, 2))

    def unpack(g, j):
        i = GROUP * g + j
        sides = []
        for ref, low, high in ((got_w, 0, 2), (got_e, 1, 3)):
            total = ref[pl.ds(i, 1)]
            total = jnp.where(block == 0, lane_roll(corner_in[low, pl.ds(g, 1)], -16 * j), total)
            total = jnp.where(block == 7, lane_roll(corner_in[high, pl.ds(g, 1)], 16 * (7 - j)), total)
            sides.append(total)
        from_west, from_east = sides
        for q in range(2):
            p = 2 * i + q
            mine = packed[pl.ds(p, 1)]
            mine = jnp.where(block == 0, lane_roll(x_ref[pl.ds(p, 1), 8:16], 8), mine)
            mine = jnp.where(block == 7, lane_roll(x_ref[pl.ds(p, 1), 64:72], 120), mine)
            a = from_west if q == 0 else lane_roll(from_west, -8)
            b = lane_roll(from_east, 8) if q == 0 else from_east
            s_ref[pl.ds(2 * p, 1)] = jnp.where(left, a, mine)
            s_ref[pl.ds(2 * p + 1, 1)] = jnp.where(left, mine, b)

    def s_north(x):
        rolled = pltpu.roll(x, 7, 1)
        return jnp.where(sub == 7, lane_roll(rolled, -16), rolled)

    def s_south(x):
        rolled = pltpu.roll(x, 1, 1)
        return jnp.where(sub == 0, lane_roll(rolled, 16), rolled)

    nothing = jnp.zeros((2, 8, LANES), F32)

    def strip_coefficients():
        def six(pair):
            return jnp.concatenate([pair] * K, 0)

        w = s_ref[2 * WET : 2 * WET + 2 * K]
        all_e = six(s_ref[2 * COEF : 2 * COEF + 2])
        all_n = six(s_ref[2 * COEF + 2 : 2 * COEF + 4])
        s_ce = all_e * w * lane_roll(w, -1)
        s_cw = lane_roll(all_e, 1) * lane_roll(w, 1) * w
        s_cn = all_n * w * s_north(w)
        s_cs = s_south(all_n) * s_south(w) * w
        s_cz = VERTICAL * (w[:-2] * w[2:])
        s_d = 1.0 - (s_ce + s_cw) - (s_cn + s_cs)
        s_d = s_d - jnp.concatenate([s_cz, nothing], 0) - jnp.concatenate([nothing, s_cz], 0)
        for i, part in enumerate((s_d, s_ce, s_cw, s_cn, s_cs)):
            s_c[i] = part
        s_c[5, 0:10] = s_cz

    def coefficients(r):
        t = pl.multiple_of(8 * r, 8)
        here, at = pl.ds(t, 8), pl.ds(t + 8, 8)
        ce, cn = x_ref[COEF : COEF + 1, at], x_ref[COEF + 1 : COEF + 2, at]
        cs = x_ref[COEF + 1 : COEF + 2, pl.ds(t + 7, 8)]
        ce = jnp.where(lane == LANES - 1, 0.0, ce)
        tiles = [x_ref[WET + k : WET + k + 1, at] for k in range(K)]
        below = None
        for k in range(K):
            wk = tiles[k]
            e = ce * (wk * lane_roll(wk, -1))
            wst = lane_roll(e, 1)
            n = cn * wk * x_ref[WET + k : WET + k + 1, pl.ds(t + 9, 8)]
            s = cs * x_ref[WET + k : WET + k + 1, pl.ds(t + 7, 8)] * wk
            d = 1.0 - (e + wst) - (n + s)
            if k < K - 1:
                z = VERTICAL * (wk * tiles[k + 1])
                c_z[k : k + 1, here] = z
                d = d - z
            if below is not None:
                d = d - below
            below = z
            c_e[k : k + 1, here] = e
            c_w[k : k + 1, here] = wst
            c_n[k : k + 1, at] = n
            diag[k : k + 1, here] = d

    edge_lane = jnp.logical_or(lane == 0, lane == LANES - 1)

    def edge_coefficients(k, carry):
        one = pl.ds(k, 1)
        faces = jnp.where(left, s_c[1, pl.ds(2 * k + 1, 1)], s_c[2, pl.ds(2 * k, 1)])
        for r in range(TILES):
            here = pl.ds(8 * r, 8)
            c = jnp.where(edge_lane, lane_roll(faces, 120 - 16 * r), 0.0)
            c_edge[one, here] = c
            diag[one, here] = diag[one, here] - c
        return carry

    def unpack_group(g, carry):
        received(strip_copies(g))
        pl.when(has_down)(lambda: received(corners_up(g)))
        pl.when(has_up)(lambda: received(corners_down(g)))
        for j in range(GROUP):
            unpack(g, j)
        return carry

    def coefficient_group(i, carry):
        @pl.when(i == 2)
        def _():
            pl.when(has_down)(lambda: received(rows_up[:1]))
            pl.when(has_up)(lambda: received(rows_down[:1]))

        pair = lax.rem(i + 1, 3) + 2 * (i // 3)
        for q in range(2):
            coefficients(2 * pair + q)
        return carry

    lax.fori_loop(0, 4, coefficient_group, 0)

    def finish_group(g, carry):
        @pl.when(g == 1)
        def _():
            strip_coefficients()
            lax.fori_loop(0, K, edge_coefficients, 0)
            pl.when(has_down)(lambda: received(rows_up[1:]))
            pl.when(has_up)(lambda: received(rows_down[1:]))

        return unpack_group(g, carry)

    lax.fori_loop(0, 2, finish_group, 0)

    pl.when(has_up)(lambda: sent(rows_up[:1]))
    pl.when(has_down)(lambda: sent(rows_down[:1]))

    def strip_product(base):
        x = s_ref[pl.ds(2 * base, 2 * K)]
        x_east, x_west = lane_roll(x, -1), lane_roll(x, 1)
        out = s_c[0] * x + (s_c[1] * x_east + s_c[2] * x_west)
        out = out + (s_c[3] * s_north(x) + s_c[4] * s_south(x))
        cz = s_c[5, 0:10]
        out = out + jnp.concatenate([cz * x[2:], nothing], 0) + jnp.concatenate([nothing, cz * x[:-2]], 0)
        return out, [jnp.where(left, x_east[2 * k + 1 : 2 * k + 2], x_west[2 * k : 2 * k + 1]) for k in range(K)]

    def product(base, edges, r, t):
        here, at = pl.ds(t, 8), pl.ds(t + 8, 8)
        north, south = pl.ds(t + 9, 8), pl.ds(t + 7, 8)
        x = [x_ref[pl.ds(base + k, 1), at] for k in range(K)]
        out = []
        for k in range(K):
            one = pl.ds(base + k, 1)
            edge = lane_roll(edges[k], 120 - 16 * r)
            p = c_e[k : k + 1, here] * lane_roll(x[k], -1) + c_w[k : k + 1, here] * lane_roll(x[k], 1)
            p = p + (c_edge[k : k + 1, here] * edge + diag[k : k + 1, here] * x[k])
            p = p + (c_n[k : k + 1, at] * x_ref[one, north] + c_n[k : k + 1, south] * x_ref[one, south])
            if k < K - 1:
                p = p + c_z[k : k + 1, here] * x[k + 1]
            if k > 0:
                p = p + c_z[k - 1 : k, here] * x[k - 1]
            out.append(p)
        return out

    def all_tiles(one):
        for r in range(TILES):
            one(r, 8 * r)

    def forward(n, carry):
        now = OTHER * lax.rem(n, 2)
        later = OTHER - now
        p, edges = strip_product(now)
        bounded = jnp.tanh(p)
        s_gain[n] = 1.0 - bounded * bounded
        s_ref[pl.ds(2 * later, 2 * K)] = bounded + s_ref[2 * SOURCE : 2 * SOURCE + 2 * K]

        def one(r, t):
            for k, p in enumerate(product(now, edges, r, t)):
                bounded = jnp.tanh(p)
                gain[n, k : k + 1, pl.ds(t, 8)] = 1.0 - bounded * bounded
                at = pl.ds(t + 8, 8)
                x_ref[pl.ds(later + k, 1), at] = bounded + x_ref[SOURCE + k : SOURCE + k + 1, at]

        all_tiles(one)
        return carry

    lax.fori_loop(0, STEPS, forward, 0)

    def turn(k, carry):
        one, o = pl.ds(k, 1), pl.ds(16, ROWS)
        final_ref[one] = x_ref[pl.ds(WET + k, 1), o] * x_ref[pl.ds(STATE + k, 1), o]
        x_ref[one, 8:72] = gain[STEPS - 1, one] * x_ref[pl.ds(COT + k, 1), 8:72]
        return carry

    lax.fori_loop(0, K, turn, 0)
    s_ref[0 : 2 * K] = s_gain[STEPS - 1] * s_ref[2 * COT : 2 * COT + 2 * K]

    def backward(m, carry):
        n = STEPS - 1 - m
        before = jnp.maximum(n - 1, 0)
        now = OTHER * lax.rem(m, 2)
        later = OTHER - now
        p, edges = strip_product(now)
        s_ref[pl.ds(2 * later, 2 * K)] = s_gain[before] * p

        def one(r, t):
            for k, p in enumerate(product(now, edges, r, t)):
                here = pl.ds(t, 8)
                adj[n, k : k + 1, here] = p
                x_ref[pl.ds(later + k, 1), pl.ds(t + 8, 8)] = gain[before, k : k + 1, here] * p

        all_tiles(one)
        return carry

    lax.fori_loop(0, STEPS, backward, 0)

    def finish(k, carry):
        one, o = pl.ds(k, 1), pl.ds(8, ROWS)
        wk = x_ref[pl.ds(WET + k, 1), 16 : 16 + ROWS]
        gini_ref[one] = wk * adj[0, one, o]
        gsrc_ref[one] = wk * (
            x_ref[pl.ds(COT + k, 1), 16 : 16 + ROWS] + adj[1, one, o] + (adj[2, one, o] + adj[3, one, o])
        )
        return carry

    lax.fori_loop(0, K, finish, 0)
    pl.when(has_up)(lambda: sent(rows_up[1:]))
    pl.when(has_down)(lambda: sent(rows_down[1:]))
    for g in range(2):
        sent(strip_copies(g))
        pl.when(has_up)(lambda: sent(corners_up(g)))
        pl.when(has_down)(lambda: sent(corners_down(g)))


def store(a_ref, b_ref, c_ref, a_out, b_out, c_out, sem):
    copies = [
        pltpu.make_async_copy(src_ref, dst_ref, sem.at[i])
        for i, (src_ref, dst_ref) in enumerate(((a_ref, a_out), (b_ref, b_out), (c_ref, c_out)))
    ]
    for copy in copies:
        copy.start()
    for copy in copies:
        copy.wait()


def body(initial_state, source, cotangent, face_coefs, land_mask, bottom):
    out = pltpu.VMEM((K, ROWS, LANES), F32)
    tiles = pltpu.VMEM((K, 8 * TILES, LANES), F32)
    pairs = pltpu.VMEM((PAIRS, 8, LANES), F32)
    steps = pltpu.VMEM((STEPS, K, 8 * TILES, LANES), F32)
    corner = pltpu.VMEM((4, 2, 8, LANES), F32)
    results = pl.pallas_call(
        kernel,
        name="window",
        out_shape=(out, out, out),
        in_specs=[pl.BlockSpec(memory_space=pl.ANY)] * 6,
        out_specs=(pl.BlockSpec(memory_space=pltpu.VMEM),) * 3,
        scratch_shapes=[
            pltpu.VMEM((PLANES + K, PAD, LANES), F32),
            pltpu.VMEM((K, ROWS, LANES), jnp.int32),
            pltpu.VMEM((ROWS, LANES), jnp.int32),
            tiles, tiles, tiles, pltpu.VMEM((K, PAD, LANES), F32), tiles, tiles,
            steps, steps,
            pltpu.VMEM((2 * PAIRS, 8, LANES), F32),
            pairs, pairs, corner, pairs, pairs, corner,
            pltpu.VMEM((2 * (PLANES + K), 8, LANES), F32),
            pltpu.VMEM((6, 2 * K, 8, LANES), F32),
            pltpu.VMEM((STEPS, 2 * K, 8, LANES), F32),
            pltpu.SemaphoreType.DMA((6,)),
            pltpu.SemaphoreType.DMA((18,)),
            pltpu.SemaphoreType.DMA((18,)),
        ],
        compiler_params=pltpu.CompilerParams(collective_id=0, has_side_effects=True),
    )(initial_state, source, cotangent, face_coefs, land_mask, bottom)
    plain = jax.ShapeDtypeStruct((K, ROWS, LANES), F32)
    return pl.pallas_call(
        store,
        name="store",
        out_shape=(plain,) * 3,
        in_specs=[pl.BlockSpec(memory_space=pltpu.VMEM)] * 3,
        out_specs=(pl.BlockSpec(memory_space=pl.ANY),) * 3,
        scratch_shapes=[pltpu.SemaphoreType.DMA((3,))],
    )(*[pltpu.with_memory_space_constraint(x, pltpu.VMEM) for x in results])


def solution(mesh):
    spec = P(None, "lat", "lon")
    return jax.shard_map(
        body,
        mesh=mesh,
        in_specs=(spec,) * 5 + (P("lat", "lon"),),
        out_specs=(spec,) * 3,
        check_vma=False,
    )
```
